32 devices in a mesh: blk: 8 (over z, y), line: 4 (over x, core).
Axes of the slice: x: 2, y: 2, z: 4, core: 2. Of those that a mesh axis runs over, the one named last changes fastest.
Arguments:
- density: float32 [8, 64, 4096], P('blk', 'line'), may hold values from 0.5 to 1.5
- momentum: float32 [8, 3, 64, 4096], P('blk', None, 'line'), may hold values from -0.5 to 0.5
- energy: float32 [8, 64, 4096], P('blk', 'line'), may hold values from 2 to 4
- adjoint: float32 [8, 5, 64, 4096], P('blk', None, 'line'), may hold values from -6 to 6
- partners: int32 [8, 4], P('blk'), may hold values from 0 to 7
- counts: int32 [8], P('blk'), may hold values from 1 to 4, as said below
- orient: int32 [8, 4], P('blk'), may hold values from 0 to 1
Outputs:
- residual: float32 [8, 5, 64, 4096], P('blk', None, 'line')
- correction: float32 [8], P('blk')
The draws below stay inside these ranges and needn't reach their ends.
Inputs may be any that keep to these rules, and one draw needn't show every extreme that they name: `partners`: slots at or past counts[b] are padding and are not read. `counts`: some block lists 4 partners.
All inputs are finite; a program needn't handle non-finite values.
Results may differ from the reference program's by a relative error of at most 0.0003.
Values sent between devices are 32-bit elements; how exact they have to be, the bound alone decides.
No kernel may reach another device: no remote copies, remote signals or barrier semaphores. Data moves between devices by JAX's collectives and lax.ppermute only.
A program may use at most 64 MiB of HBM per device.

```python
import jax
import jax.numpy as jnp
from jax import lax

NY = 4096
PMAX = 4
NX = 64
BLOCKS = 8


def draw_counts(key, part):
    first_key, second_key = jax.random.split(jax.random.fold_in(key, 17))
    drawn = jax.random.randint(first_key, (BLOCKS,), 1, PMAX + 1, dtype=jnp.int32)
    chosen = jax.random.randint(second_key, (), 0, BLOCKS, dtype=jnp.int32)
    return jnp.where(jnp.arange(BLOCKS, dtype=jnp.int32) == chosen, PMAX, drawn).astype(jnp.int32)


def with_ends(values, rng, least, high):
    dims = values.shape
    index_at = [jax.random.randint(jax.random.fold_in(rng, axis), (), 0, dims[axis]) for axis in range(len(dims))]
    values = values.at[tuple(index_at)].set(least)
    longest = dims.index(max(dims))
    index_at[longest] = (index_at[longest] + 1) % dims[longest]
    return values.at[tuple(index_at)].set(high)


def block_scale(rng, shape, cuts, least, top_value):
    factor_of = 1.0
    for axis_at, blocks in cuts:
        steps = jax.random.uniform(jax.random.fold_in(jax.random.fold_in(rng, 6), axis_at), (blocks,), jnp.float32, least / len(cuts), top_value / len(cuts))
        factor_of = factor_of * jnp.repeat(jnp.exp(steps), shape[axis_at] // blocks).reshape((-1,) + (1,) * (len(shape) - 1 - axis_at))
    return factor_of


def gaussian(stream_key, dims, width, most, cuts=(), kind=jnp.bfloat16):
    factor_of = block_scale(stream_key, dims, cuts, -0.22, 0.18) if cuts else 1.0
    values = jax.random.normal(stream_key, dims, jnp.float32) * width * factor_of
    return jnp.minimum(jnp.maximum(values, -most), most).astype(kind)


def setup_inputs(seed: int = 0) -> dict:
    streams_of = jax.random.split(jax.random.key(seed), 8)
    return {
        "density": jnp.clip(0.5 + 1.0 * jax.random.uniform(streams_of[0], (BLOCKS, NX, NY), jnp.float32) ** block_scale(streams_of[0], (BLOCKS, NX, NY), ((0, 8), (1, 4)), -0.2, 0.2), 0.5, 1.5),
        "momentum": jnp.clip(jax.random.uniform(streams_of[1], (BLOCKS, 3, NX, NY), jnp.float32, -0.5, 0.5) * block_scale(streams_of[1], (BLOCKS, 3, NX, NY), ((0, 8), (2, 4)), -0.4, 0.0), -0.5, 0.5),
        "energy": jnp.clip(2.0 + 2.0 * jax.random.uniform(streams_of[2], (BLOCKS, NX, NY), jnp.float32) ** block_scale(streams_of[2], (BLOCKS, NX, NY), ((0, 8), (1, 4)), -0.2, 0.2), 2.0, 4.0),
        "adjoint": gaussian(streams_of[3], (BLOCKS, 5, NX, NY), 1.0, 6.0, ((0, 8), (2, 4)), jnp.float32),
        "partners": with_ends(jax.random.randint(streams_of[4], (BLOCKS, PMAX), 0, BLOCKS), jax.random.fold_in(streams_of[4], 1), 0, BLOCKS - 1).astype(jnp.int32),
        "counts": draw_counts(jax.random.fold_in(streams_of[7], 71), 0),
        "orient": with_ends(jax.random.randint(streams_of[6], (BLOCKS, PMAX), 0, 2), jax.random.fold_in(streams_of[6], 1), 0, 1).astype(jnp.int32),
    }


stencil_one = 0.75
stencil_two = -0.15
stencil_three = 1.0 / 60.0
gamma_less = 0.4
viscosity = 0.5
conduction = 1.5
penalty = 4.0


def difference(fields, direction, start_row, extent):
    length = fields.shape[direction]

    def shifted(offset):
        return lax.slice_in_dim(fields, 3 + offset, length - 3 + offset, axis=direction)

    shape_list = [1] * fields.ndim
    shape_list[direction] = length - 6
    global_row = (start_row + 3 + jnp.arange(length - 6, dtype=jnp.int32)).reshape(shape_list)
    central_one = shifted(1) - shifted(-1)
    central_two = shifted(2) - shifted(-2)
    central_three = shifted(3) - shifted(-3)
    interior = stencil_one * central_one + stencil_two * central_two + stencil_three * central_three
    fourth = (2.0 / 3.0) * central_one - (1.0 / 12.0) * central_two
    second = 0.5 * central_one
    forward = shifted(1) - shifted(0)
    backward = shifted(0) - shifted(-1)
    result = jnp.where((global_row == 2) | (global_row == extent - 3), fourth, interior)
    result = jnp.where((global_row == 1) | (global_row == extent - 2), second, result)
    result = jnp.where(global_row == 0, forward, result)
    result = jnp.where(global_row == extent - 1, backward, result)
    return result


def primitives(fields):
    density_raw = fields[:, 0:1]
    density_safe = jnp.where(density_raw == 0.0, 1.0, density_raw)
    velocity = fields[:, 1:4] / density_safe
    kinetic = 0.5 * jnp.sum(fields[:, 1:4] * velocity, axis=1, keepdims=True)
    pressure = gamma_less * (fields[:, 4:5] - kinetic)
    return velocity, pressure, density_safe


def direction_residual(fields, direction, start_row, extent, normal_index):
    velocity, pressure, density_safe = primitives(fields)
    primitive = jnp.concatenate([velocity, pressure / density_safe], axis=1)
    gradient = difference(primitive, direction, start_row, extent)
    length = fields.shape[direction]
    middle = lax.slice_in_dim(fields, 3, length - 3, axis=direction)
    mid_velocity = lax.slice_in_dim(velocity, 3, length - 3, axis=direction)
    mid_pressure = lax.slice_in_dim(pressure, 3, length - 3, axis=direction)
    normal_speed = mid_velocity[:, normal_index:normal_index + 1]
    selector = (jnp.arange(3) == normal_index).astype(fields.dtype).reshape(1, 3, 1, 1)
    convective = jnp.concatenate([middle[:, normal_index + 1:normal_index + 2], middle[:, 1:4] * normal_speed + mid_pressure * selector, (middle[:, 4:5] + mid_pressure) * normal_speed], axis=1)
    viscous = jnp.concatenate([jnp.zeros_like(normal_speed), viscosity * gradient[:, 0:3], (viscosity * conduction) * gradient[:, 3:4]], axis=1)
    return difference(convective - viscous, direction, start_row + 3, extent)


def reference(density, momentum, energy, adjoint, partners, counts, orient):
    bottoms = jnp.concatenate([density[:, None, :, 0], momentum[:, :, :, 0], energy[:, None, :, 0]], axis=1)
    slots = jnp.arange(PMAX, dtype=jnp.int32)
    weights = jnp.where(slots[None, :] < counts[:, None], 1.0 / counts[:, None].astype(jnp.float32), jnp.float32(0.0)).astype(jnp.float32)
    signs = jnp.ones((BLOCKS, PMAX, 5), jnp.float32).at[:, :, 2].set(1.0 - 2.0 * orient.astype(jnp.float32))
    rows = bottoms[partners]
    target = jnp.sum((rows * weights[:, :, None, None]) * signs[:, :, :, None], axis=1)

    def one_block(pieces):
        block_density, block_momentum, block_energy, block_adjoint, block_target = pieces
        state = jnp.concatenate([block_density[None, None], block_momentum[None], block_energy[None, None]], axis=1)
        padded_x = jnp.pad(state, ((0, 0), (0, 0), (6, 6), (0, 0)))
        padded_y = jnp.pad(state, ((0, 0), (0, 0), (0, 0), (6, 6)))
        xpart = direction_residual(padded_x, 2, -6, NX, 0)
        ypart = direction_residual(padded_y, 3, -6, NY, 1)
        result = xpart + ypart
        result = result.at[:, :, :, NY - 1].add(penalty * (state[:, :, :, NY - 1] - block_target[None]))
        return result[0], jnp.sum(block_adjoint * result[0])

    residual, partial_sums = lax.map(one_block, (density, momentum, energy, adjoint, target))
    correction = (partial_sums / (NX * NY)).astype(jnp.float32)
    return residual, correction
```

```python
import functools

import jax
import jax.numpy as jnp
from jax import lax
from jax.experimental import pallas as pl
from jax.experimental.pallas import tpu as pltpu
from jax.sharding import PartitionSpec as P

STENCIL = (0.75, -0.15, 1.0 / 60.0)
gamma_less = 0.4
viscosity = 0.5
conduction = 1.5
penalty = 4.0
LANES = 128
SUB = 8
CHUNK = 4
F32 = jnp.float32
VMEM_LIMIT = 20 * 1024 * 1024

_ONE = {k: STENCIL[k - 1] for k in (1, 2, 3)}
_ONE.update({-k: -STENCIL[k - 1] for k in (1, 2, 3)})
TWICE = [sum(_ONE[a] * _ONE[b] for a in _ONE for b in _ONE if a + b == m) for m in range(7)]


def tile_iota(axis):
    return lax.broadcasted_iota(jnp.int32, (SUB, LANES), axis)


def coefficients(index, extent):
    inside = (index >= 0) & (index < extent)
    end = (index == 0) | (index == extent - 1)
    second = (index == 1) | (index == extent - 2)
    fourth = (index == 2) | (index == extent - 3)
    one = jnp.where(fourth, 2.0 / 3.0, jnp.where(second, 0.5, jnp.where(end, 1.0, STENCIL[0])))
    two = jnp.where(fourth, -1.0 / 12.0, jnp.where(second | end, 0.0, STENCIL[1]))
    three = jnp.where(fourth | second | end, 0.0, STENCIL[2])
    point = jnp.where(index == 0, -1.0, jnp.where(index == extent - 1, 1.0, 0.0))
    return [jnp.where(inside, c, 0.0).astype(F32) for c in (one, two, three, point)]


def load_state(refs, rt, t):
    density, momentum, energy = refs
    rows = slice(rt * SUB, (rt + 1) * SUB)
    cols = pl.ds(t * LANES if isinstance(t, int) else pl.multiple_of(t * LANES, LANES), LANES)
    return [density[rows, cols]] + [momentum[a, rows, cols] for a in range(3)] + [energy[rows, cols]]


def primitive_of(state):
    rho, m0, m1, m2, e = state
    inv = 1.0 / rho
    u = [m0 * inv, m1 * inv, m2 * inv]
    p = gamma_less * (e - 0.5 * (m0 * u[0] + m1 * u[1] + m2 * u[2]))
    return u, p, p * inv


def convective(state, u, p, d):
    n = u[d]
    out = [state[1 + d]]
    for a in range(3):
        f = state[1 + a] * n
        out.append(f + p if a == d else f)
    out.append((state[4] + p) * n)
    return out


def contribution(state, up):
    u, p, temp = primitive_of(state)
    conv = convective(state, u, p, 0)
    row = tile_iota(0)
    shift = (lambda x, m: pltpu.roll(x, m, 0)) if up else (lambda x, m: pltpu.roll(x, SUB - m, 0))
    sign = -1.0 if up else 1.0
    keep = [None] + [(row < m) if up else (row >= SUB - m) for m in range(1, 7)]
    out = []
    for var in range(5):
        acc = None
        for m in (1, 2, 3):
            term = shift(conv[var], m) * jnp.where(keep[m], sign * STENCIL[m - 1], 0.0)
            acc = term if acc is None else acc + term
        if var:
            prim = u[var - 1] if var < 4 else temp
            scale = -viscosity * (conduction if var == 4 else 1.0)
            for m in range(1, 7):
                acc = acc + shift(prim, m) * jnp.where(keep[m], scale * TWICE[m], 0.0)
        out.append(acc)
    mass, first, second = out[0], out[1], out[2]
    if up:
        first = jnp.where(row >= 6, pltpu.roll(mass, 6, 0), first)
        second = jnp.where(row == 6, pltpu.roll(mass, 4, 0), second)
    else:
        first = jnp.where(row < 2, pltpu.roll(mass, 3, 0), first)
        second = jnp.where(row == 0, pltpu.roll(mass, 1, 0), second)
    return [first, second, out[3], out[4]]


def unpack(tiles, up):
    row = tile_iota(0)
    first, second, third, fourth = tiles
    if up:
        mass = jnp.where(row < 2, pltpu.roll(first, 2, 0), 0.0) + jnp.where(row == 2, pltpu.roll(second, 4, 0), 0.0)
        keep = row < 6
    else:
        mass = jnp.where((row == 5) | (row == 6), pltpu.roll(first, 5, 0), 0.0) + jnp.where(
            row == 7, pltpu.roll(second, 7, 0), 0.0)
        keep = row >= 2
    return [mass] + [jnp.where(keep, x, 0.0) for x in (first, second, third, fourth)]


def pack_kernel(across, density, momentum, energy, out_ref, *rest):
    refs = (density, momentum, energy)
    tiles = density.shape[1] // LANES
    row_tiles = density.shape[0] // SUB
    odd = lax.rem(lax.axis_index("line"), 2)

    def side(up):
        rt = row_tiles - 1 if up else 0

        def body(t, carry):
            cols = pl.ds(pl.multiple_of(t * LANES, LANES), LANES)
            for n, x in enumerate(contribution(load_state(refs, rt, t), up)):
                out_ref[n, :, cols] = x
            return carry

        lax.fori_loop(0, tiles, body, 0, unroll=2)

    up_when = 1 if across else 0

    @pl.when(odd == up_when)
    def _():
        side(True)

    @pl.when(odd != up_when)
    def _():
        side(False)

    if rest:
        (slots,) = rest
        width = slot_width(row_tiles)
        per = LANES // width
        block = lax.axis_index("blk")
        lane = tile_iota(1)
        base = lax.rem(block, per) * width
        value = jnp.zeros((SUB, LANES), F32)
        for rt in range(row_tiles):
            for var, x in enumerate(load_state(refs, rt, 0)):
                value = jnp.where(lane == base + (var * row_tiles + rt), x[:, 0:1], value)
        for n in range(slots.shape[0]):
            slots[n] = jnp.where(block // per == n, value, 0.0)


def slot_width(row_tiles):
    width = 1
    while width < 5 * row_tiles:
        width *= 2
    return width


def whole():
    return pl.BlockSpec(memory_space=pltpu.VMEM)


def params():
    return pltpu.CompilerParams(vmem_limit_bytes=VMEM_LIMIT)


def lane_shifts(tiles):
    lane = tile_iota(1)
    count = len(tiles) - 2
    got = [{0: tiles[j + 1]} for j in range(count)]
    for k in (1, 2, 3):
        ahead = [pltpu.roll(x, LANES - k, 1) for x in tiles[1:]]
        behind = [pltpu.roll(x, k, 1) for x in tiles[:-1]]
        for j in range(count):
            got[j][k] = jnp.where(lane < LANES - k, ahead[j], ahead[j + 1])
            got[j][-k] = jnp.where(lane >= k, behind[j + 1], behind[j])
    return got


def apply(weights, at):
    one, two, three, point = weights
    return one * (at(1) - at(-1)) + two * (at(2) - at(-2)) + three * (at(3) - at(-3)) + point * at(0)


def flux_kernel(density, momentum, energy, fy_ref, xd_ref, prim, press, fx, xcoef, ycoef):
    refs = (density, momentum, energy)
    rows, cols = density.shape
    row_tiles, tiles = rows // SUB, cols // LANES
    line = lax.axis_index("line")
    extent = rows * lax.axis_size("line")
    zero = jnp.zeros((SUB, LANES), F32)

    for g in range(row_tiles + 1):
        for c, w in enumerate(coefficients(line * rows - 3 + g * SUB + tile_iota(0), extent)):
            xcoef[0, g, c] = w
    for r in range(row_tiles):
        for c, w in enumerate(coefficients(line * rows + r * SUB + tile_iota(0), extent)):
            xcoef[1, r, c] = w
    for n, start in enumerate((0, LANES, cols - LANES)):
        for c, w in enumerate(coefficients(start + tile_iota(1), cols)):
            ycoef[n, c] = w

    for var in range(5):
        for r in range(row_tiles):
            fy_ref[var, 0, r * SUB:(r + 1) * SUB, :] = zero
            fy_ref[var, tiles + 1, r * SUB:(r + 1) * SUB, :] = zero
    for var in range(4):
        for r in range(row_tiles + 2):
            prim[var, 0, r * SUB:(r + 1) * SUB, :] = zero
            prim[var, tiles + 1, r * SUB:(r + 1) * SUB, :] = zero
    for j in range(CHUNK):
        for r in range(row_tiles + 1):
            fx[j, 0, r * SUB:(r + 1) * SUB, :] = zero

    def first(t, carry):
        for rt in range(row_tiles):
            u, p, temp = primitive_of(load_state(refs, rt, t))
            at = slice((rt + 1) * SUB, (rt + 2) * SUB)
            for var, x in enumerate(u + [temp]):
                prim[var, t + 1, at, :] = x
            press[t, rt * SUB:(rt + 1) * SUB, :] = p
        for var in range(4):
            prim[var, t + 1, 0:SUB, :] = zero
            prim[var, t + 1, (row_tiles + 1) * SUB:(row_tiles + 2) * SUB, :] = zero
        return carry

    lax.fori_loop(0, tiles, first, 0, unroll=2)

    def second(step, carry):
        t0 = step * CHUNK
        for rt in range(row_tiles):
            at = slice((rt + 1) * SUB, (rt + 2) * SUB)
            own = slice(rt * SUB, (rt + 1) * SUB)
            grads = []
            for var in range(4):
                window = [prim[var, t0 + j, at, :] for j in range(CHUNK + 2)]
                shifted = lane_shifts(window)
                scale = viscosity * (conduction if var == 3 else 1.0)
                line_of = []
                for j in range(CHUNK):
                    which = jnp.where(t0 + j == 0, 0, jnp.where(t0 + j == tiles - 1, 2, 1))
                    w = [ycoef[which, c] for c in range(4)]
                    line_of.append(scale * apply(w, lambda k, j=j: shifted[j][k]))
                grads.append(line_of)
            for j in range(CHUNK):
                t = t0 + j
                state = load_state(refs, rt, t)
                u = [prim[a, t + 1, at, :] for a in range(3)]
                p = press[t, own, :]
                for var, f in enumerate(convective(state, u, p, 1)):
                    fy_ref[var, t + 1, own, :] = f - grads[var - 1][j] if var else f
        for j in range(CHUNK):
            t = t0 + j
            for var in range(4):
                scale = -viscosity * (conduction if var == 3 else 1.0)
                for g in range(row_tiles + 1):
                    w = [xcoef[0, g, c] for c in range(4)]
                    base = SUB - 3 + g * SUB
                    fx[j, var + 1, g * SUB:(g + 1) * SUB, :] = scale * apply(
                        w, lambda k: prim[var, t + 1, base + k:base + k + SUB, :])
            for rt in range(row_tiles):
                at = slice((rt + 1) * SUB, (rt + 2) * SUB)
                own = slice(rt * SUB, (rt + 1) * SUB)
                state = load_state(refs, rt, t)
                u = [prim[a, t + 1, at, :] for a in range(3)]
                for var, f in enumerate(convective(state, u, press[t, own, :], 0)):
                    place = slice(3 + rt * SUB, 3 + (rt + 1) * SUB)
                    fx[j, var, place, :] = fx[j, var, place, :] + f if var else f
            for var in range(5):
                for rt in range(row_tiles):
                    w = [xcoef[1, rt, c] for c in range(4)]
                    base = 3 + rt * SUB
                    xd_ref[var, t, rt * SUB:(rt + 1) * SUB, :] = apply(
                        w, lambda k: fx[j, var, base + k:base + k + SUB, :])
        return carry

    lax.fori_loop(0, tiles // CHUNK, second, 0)


def volume_kernel(density, momentum, energy, adjoint, fy, xd, res_ref, sum_ref, ycoef):
    refs = (density, momentum, energy)
    rows, cols = density.shape
    row_tiles, tiles = rows // SUB, cols // LANES
    for n, start in enumerate((0, LANES, cols - LANES)):
        for c, w in enumerate(coefficients(start + tile_iota(1), cols)):
            ycoef[n, c] = w

    def body(step, acc):
        t0 = step * CHUNK
        for rt in range(row_tiles):
            own = slice(rt * SUB, (rt + 1) * SUB)
            for var in range(5):
                shifted = lane_shifts([fy[var, t0 + j, own, :] for j in range(CHUNK + 2)])
                for j in range(CHUNK):
                    t = t0 + j
                    which = jnp.where(t == 0, 0, jnp.where(t == tiles - 1, 2, 1))
                    w = [ycoef[which, c] for c in range(4)]
                    r = xd[var, t, own, :] + apply(w, lambda k: shifted[j][k])
                    res_ref[var, t, own, :] = r
                    acc = acc + adjoint[var, own, pl.ds(pl.multiple_of(t * LANES, LANES), LANES)] * r
        return acc

    acc = lax.fori_loop(0, tiles // CHUNK, body, jnp.zeros((SUB, LANES), F32))
    last = tiles - 1
    weight = jnp.where(tile_iota(1) == LANES - 1, penalty, 0.0)
    for rt in range(row_tiles):
        own = slice(rt * SUB, (rt + 1) * SUB)
        for var, x in enumerate(load_state(refs, rt, last)):
            extra = weight * x
            res_ref[var, last, own, :] = res_ref[var, last, own, :] + extra
            acc = acc + adjoint[var, own, last * LANES:] * extra
    sum_ref[...] = acc


def border_kernel(partners, counts, orient, chip, across, slots, res, adjoint, total, out_ref, sum_ref):
    rows, cols = adjoint.shape[1:]
    row_tiles, tiles = rows // SUB, cols // LANES
    odd = lax.rem(lax.axis_index("line"), 2) == 1

    def body(t, acc):
        at = pl.ds(pl.multiple_of(t * LANES, LANES), LANES)
        near = [chip[n, :, at] for n in range(4)]
        far = [across[n, :, at] for n in range(4)]
        below = unpack([jnp.where(odd, a, b) for a, b in zip(near, far)], True)
        above = unpack([jnp.where(odd, b, a) for a, b in zip(near, far)], False)
        for var in range(5):
            for rt in range(row_tiles):
                own = slice(rt * SUB, (rt + 1) * SUB)
                r = res[var, t, own, :]
                for there, extra in ((0, below[var]), (row_tiles - 1, above[var])):
                    if rt == there:
                        r = r + extra
                        acc = acc + adjoint[var, own, at] * extra
                out_ref[var, own, at] = r
        return acc

    acc = lax.fori_loop(0, tiles, body, total[...], unroll=2)

    width = slot_width(row_tiles)
    per = LANES // width
    lane = tile_iota(1)
    count = counts[0]
    share = 1.0 / jnp.full((SUB, LANES), count).astype(F32)
    flipped = (lane % width) // row_tiles == 2
    target = jnp.zeros((SUB, LANES), F32)
    for n in range(slots.shape[0]):
        weight = jnp.zeros((SUB, LANES), F32)
        for k in range(partners.shape[1]):
            turn = 1.0 - 2.0 * jnp.full((SUB, LANES), orient[0, k]).astype(F32)
            hit = (lane // width + n * per == partners[0, k]) & (k < count)
            weight = weight + jnp.where(hit, share * jnp.where(flipped, turn, 1.0), 0.0)
        target = target + weight * slots[n]
    step = width
    while step < LANES:
        target = target + pltpu.roll(target, step, 1)
        step *= 2
    for var in range(5):
        for rt in range(row_tiles):
            own = slice(rt * SUB, (rt + 1) * SUB)
            moved = pltpu.roll(target, LANES - 1 - (var * row_tiles + rt), 1)
            extra = jnp.where(lane == LANES - 1, -penalty * moved, 0.0)
            cut = slice((tiles - 1) * LANES, tiles * LANES)
            out_ref[var, own, cut] = out_ref[var, own, cut] + extra
            acc = acc + adjoint[var, own, cut] * extra
    sum_ref[...] = jnp.full((SUB, LANES), jnp.sum(acc))


def per_device(density, momentum, energy, adjoint, partners, counts, orient):
    rows, cols = density.shape[1:]
    row_tiles, tiles = rows // SUB, cols // LANES
    lines, blocks = lax.axis_size("line"), lax.axis_size("blk")
    state = (density[0], momentum[0], energy[0])
    shape = jax.ShapeDtypeStruct
    pieces = -(-blocks * slot_width(row_tiles) // LANES)
    packed = shape((4, SUB, cols), F32)

    def pack(is_across):
        outs = [packed, shape((pieces, SUB, LANES), F32)] if is_across else [packed]
        return pl.pallas_call(
            functools.partial(pack_kernel, is_across), out_shape=outs,
            in_specs=[whole()] * 3, out_specs=[whole()] * len(outs), compiler_params=params(),
            cost_estimate=pl.CostEstimate(flops=10**6, bytes_accessed=3 * 10**6, transcendentals=0),
        )(*state)

    send_far, slots = pack(True)
    (send_near,) = pack(False)
    far = lax.ppermute(send_far, "line", [p for i in range(1, lines - 1, 2) for p in ((i, i + 1), (i + 1, i))])
    near = lax.ppermute(send_near, "line", [(i, i ^ 1) for i in range(lines)])
    hop = 1
    while hop < blocks:
        slots = slots + lax.ppermute(slots, "blk", [(i, i ^ hop) for i in range(blocks)])
        hop *= 2

    fy, xd = pl.pallas_call(
        flux_kernel,
        out_shape=[shape((5, tiles + 2, rows, LANES), F32), shape((5, tiles, rows, LANES), F32)],
        in_specs=[whole()] * 3, out_specs=[whole()] * 2,
        scratch_shapes=[
            pltpu.VMEM((4, tiles + 2, rows + 2 * SUB, LANES), F32),
            pltpu.VMEM((tiles, rows, LANES), F32),
            pltpu.VMEM((CHUNK, 5, rows + SUB, LANES), F32),
            pltpu.VMEM((2, row_tiles + 1, 4, SUB, LANES), F32),
            pltpu.VMEM((3, 4, SUB, LANES), F32),
        ],
        compiler_params=params(),
        cost_estimate=pl.CostEstimate(flops=10**8, bytes_accessed=10**7, transcendentals=0),
    )(*state)
    res, total = pl.pallas_call(
        volume_kernel,
        out_shape=[shape((5, tiles, rows, LANES), F32), shape((SUB, LANES), F32)],
        in_specs=[whole()] * 6, out_specs=[whole()] * 2,
        scratch_shapes=[pltpu.VMEM((3, 4, SUB, LANES), F32)],
        compiler_params=params(),
        cost_estimate=pl.CostEstimate(flops=10**8, bytes_accessed=10**7, transcendentals=0),
    )(*state, adjoint[0], fy, xd)
    smem = pl.BlockSpec(memory_space=pltpu.SMEM)
    result, part = pl.pallas_call(
        border_kernel,
        out_shape=[shape((5, rows, cols), F32), shape((SUB, LANES), F32)],
        in_specs=[smem] * 3 + [whole()] * 6, out_specs=[whole()] * 2,
        compiler_params=params(),
        cost_estimate=pl.CostEstimate(flops=10**6, bytes_accessed=4 * 10**6, transcendentals=0),
    )(partners, counts, orient, near, far, slots, res, adjoint[0], total)
    whole_sum = part
    if lines <= 4:
        for s in range(1, lines):
            whole_sum = whole_sum + lax.ppermute(part, "line", [(i, (i + s) % lines) for i in range(lines)])
    else:
        whole_sum = lax.psum(part, "line")
    correction = whole_sum[0, 0:1] / (rows * lines * cols)
    return result[None], correction


def solution(mesh):
    return jax.shard_map(
        per_device,
        mesh=mesh,
        in_specs=(
            P("blk", "line", None),
            P("blk", None, "line", None),
            P("blk", "line", None),
            P("blk", None, "line", None),
            P("blk", None),
            P("blk"),
            P("blk", None),
        ),
        out_specs=(P("blk", None, "line", None), P("blk")),
        check_vma=False,
    )
```

```python
import jax
import jax.numpy as jnp
from jax import lax
from jax.experimental import pallas as pl
from jax.experimental.pallas import tpu as pltpu
from jax.sharding import PartitionSpec as P


STENCIL = (0.75, -0.15, 1.0 / 60.0)
gamma_less = 0.4
viscosity = 0.5
conduction = 1.5
penalty = 4.0
LANES = 128
SUB = 8
CHUNK = 4
WIDE = 4
F32 = jnp.float32
VMEM_LIMIT = 20 * 1024 * 1024

_ONE = {k: STENCIL[k - 1] for k in (1, 2, 3)}
_ONE.update({-k: -STENCIL[k - 1] for k in (1, 2, 3)})
TWICE = [sum(_ONE[a] * _ONE[b] for a in _ONE for b in _ONE if a + b == m) for m in range(7)]


def tile_iota(axis):
    return lax.broadcasted_iota(jnp.int32, (SUB, LANES), axis)


def coefficients(index, extent):
    inside = (index >= 0) & (index < extent)
    end = (index == 0) | (index == extent - 1)
    second = (index == 1) | (index == extent - 2)
    fourth = (index == 2) | (index == extent - 3)
    one = jnp.where(fourth, 2.0 / 3.0, jnp.where(second, 0.5, jnp.where(end, 1.0, STENCIL[0])))
    two = jnp.where(fourth, -1.0 / 12.0, jnp.where(second | end, 0.0, STENCIL[1]))
    three = jnp.where(fourth | second | end, 0.0, STENCIL[2])
    point = jnp.where(index == 0, -1.0, jnp.where(index == extent - 1, 1.0, 0.0))
    return [jnp.where(inside, c, 0.0).astype(F32) for c in (one, two, three, point)]


def load_state(refs, rt, t):
    density, momentum, energy = refs
    rows = slice(rt * SUB, (rt + 1) * SUB)
    cols = pl.ds(t * LANES if isinstance(t, int) else pl.multiple_of(t * LANES, LANES), LANES)
    return [density[rows, cols]] + [momentum[a, rows, cols] for a in range(3)] + [energy[rows, cols]]


def primitive_of(state):
    rho, m0, m1, m2, e = state
    inv = 1.0 / rho
    u = [m0 * inv, m1 * inv, m2 * inv]
    p = gamma_less * (e - 0.5 * (m0 * u[0] + m1 * u[1] + m2 * u[2]))
    return u, p, p * inv


def convective(state, u, p, d):
    n = u[d]
    out = [state[1 + d]]
    for a in range(3):
        f = state[1 + a] * n
        out.append(f + p if a == d else f)
    out.append((state[4] + p) * n)
    return out


def contribution(state, up):
    u, p, temp = primitive_of(state)
    conv = convective(state, u, p, 0)
    row = tile_iota(0)
    shift = (lambda x, m: pltpu.roll(x, m, 0)) if up else (lambda x, m: pltpu.roll(x, SUB - m, 0))
    sign = -1.0 if up else 1.0
    keep = [None] + [(row < m) if up else (row >= SUB - m) for m in range(1, 7)]
    out = []
    for var in range(5):
        acc = None
        for m in (1, 2, 3):
            term = shift(conv[var], m) * jnp.where(keep[m], sign * STENCIL[m - 1], 0.0)
            acc = term if acc is None else acc + term
        if var:
            prim = u[var - 1] if var < 4 else temp
            scale = -viscosity * (conduction if var == 4 else 1.0)
            for m in range(1, 7):
                acc = acc + shift(prim, m) * jnp.where(keep[m], scale * TWICE[m], 0.0)
        out.append(acc)
    mass, first, second = out[0], out[1], out[2]
    if up:
        first = jnp.where(row >= 6, pltpu.roll(mass, 6, 0), first)
        second = jnp.where(row == 6, pltpu.roll(mass, 4, 0), second)
    else:
        first = jnp.where(row < 2, pltpu.roll(mass, 3, 0), first)
        second = jnp.where(row == 0, pltpu.roll(mass, 1, 0), second)
    return [first, second, out[3], out[4]]


def unpack(tiles, up):
    row = tile_iota(0)
    first, second, third, fourth = tiles
    if up:
        mass = jnp.where(row < 2, pltpu.roll(first, 2, 0), 0.0) + jnp.where(row == 2, pltpu.roll(second, 4, 0), 0.0)
        keep = row < 6
    else:
        mass = jnp.where((row == 5) | (row == 6), pltpu.roll(first, 5, 0), 0.0) + jnp.where(
            row == 7, pltpu.roll(second, 7, 0), 0.0)
        keep = row >= 2
    return [mass] + [jnp.where(keep, x, 0.0) for x in (first, second, third, fourth)]


def side_of(refs, up, out_ref, rt, first, last):
    def body(t, carry):
        cols = pl.ds(pl.multiple_of(t * LANES, LANES), LANES)
        for n, x in enumerate(contribution(load_state(refs, rt, t), up)):
            out_ref[n, :, cols] = x
        return carry

    lax.fori_loop(first, last, body, 0, unroll=2)


def by_parity(up_when, run):
    odd = lax.rem(lax.axis_index("line"), 2)

    @pl.when(odd == up_when)
    def _():
        run(True)

    @pl.when(odd != up_when)
    def _():
        run(False)


def pack_kernel(density, momentum, energy, out_ref, slots, buf, other, sems):
    rows, cols = density.shape
    row_tiles, tiles = rows // SUB, cols // LANES
    up = lax.rem(lax.axis_index("line"), 2) == 1
    mine = jnp.where(up, row_tiles - 1, 0)
    sources = [density] + [momentum.at[a] for a in range(3)] + [energy]
    halves = 2
    part = cols // halves
    copies = []
    for h in range(halves):
        for n, x in enumerate(sources):
            at = pl.ds(pl.multiple_of(mine * SUB, SUB), SUB)
            copies.append(pltpu.make_async_copy(
                x.at[at, pl.ds(h * part, part)], buf.at[n, :, pl.ds(h * part, part)], sems.at[h, n]))
    bottom = [pltpu.make_async_copy(x.at[:, pl.ds(0, LANES)], other.at[n], sems.at[halves, n])
              for n, x in enumerate(sources)]
    for c in copies + bottom:
        c.start()

    refs = (buf.at[0], buf.at[1:4], buf.at[4])
    for h in range(halves):
        for c in copies[h * 5:(h + 1) * 5]:
            c.wait()
        by_parity(1, lambda up_side: side_of(refs, up_side, out_ref, 0, h * tiles // halves, (h + 1) * tiles // halves))

    for c in bottom:
        c.wait()
    width = slot_width(row_tiles)
    per = LANES // width
    block = lax.axis_index("blk")
    lane = tile_iota(1)
    base = lax.rem(block, per) * width
    value = jnp.zeros((SUB, LANES), F32)
    for rt in range(row_tiles):
        for var in range(5):
            x = other[var, rt * SUB:(rt + 1) * SUB, 0:1]
            value = jnp.where(lane == base + (var * row_tiles + rt), x, value)
    for n in range(slots.shape[0]):
        slots[n] = jnp.where(block // per == n, value, 0.0)


def slot_width(row_tiles):
    width = 1
    while width < 5 * row_tiles:
        width *= 2
    return width


def whole():
    return pl.BlockSpec(memory_space=pltpu.VMEM)


def params():
    return pltpu.CompilerParams(vmem_limit_bytes=VMEM_LIMIT)


def lane_weights(ref, cols):
    for n, start in enumerate((0, LANES, cols - LANES)):
        at = start + tile_iota(1)
        one, _, _, point = coefficients(at, cols)
        for c, w in enumerate((one, point)
                              + tuple(coefficients(at - 2, cols)[1:3]) + tuple(coefficients(at + 2, cols)[1:3])):
            ref[n, c] = w


def lane_difference(tiles, weights):
    lane = tile_iota(1)
    count = len(tiles) - 2

    def shift(values, k):
        return [pltpu.roll(x, (LANES - k) % LANES, 1) for x in values]

    ahead = shift(tiles[1:], 1)
    behind = shift(tiles[:-1], -1)
    plus = [jnp.where(lane < LANES - 1, ahead[j], ahead[j + 1]) for j in range(count)]
    minus = [jnp.where(lane >= 1, behind[j + 1], behind[j]) for j in range(count)]
    far = [weights(j + 1, 2) * v + weights(j + 1, 3) * p
           for j, (v, p) in enumerate(zip(tiles[1:], plus + [ahead[count]]))]
    back = [weights(j, 4) * v + weights(j, 5) * m for j, (v, m) in enumerate(zip(tiles[:-1], [behind[0]] + minus))]
    far, back = shift(far, 2), shift(back, -2)
    out = []
    for j in range(count):
        f = jnp.where(lane < LANES - 2, far[j], far[j + 1])
        b = jnp.where(lane >= 2, back[j + 1], back[j])
        out.append((weights(j + 1, 0) * (plus[j] - minus[j]) + weights(j + 1, 1) * tiles[j + 1]) + (f - b))
    return out


def weights_at(ref, t0, tiles):
    which = [jnp.where(t0 + j - 1 <= 0, 0, jnp.where(t0 + j - 1 >= tiles - 1, 2, 1)) for j in range(WIDE + 2)]
    return lambda j, c: ref[which[j], c]


def apply(weights, at):
    one, two, three, point = weights
    return one * (at(1) - at(-1)) + two * (at(2) - at(-2)) + three * (at(3) - at(-3)) + point * at(0)


def interior(at):
    one, two, three = STENCIL
    return one * (at(1) - at(-1)) + two * (at(2) - at(-2)) + three * (at(3) - at(-3))


def first_kernel(density, momentum, energy, lists,
                 prim, press, xd_ref, near_ref, mix_ref, fx, xcoef):
    refs = (density, momentum, energy)
    rows, cols = density.shape
    row_tiles, tiles = rows // SUB, cols // LANES
    line = lax.axis_index("line")
    extent = rows * lax.axis_size("line")
    zero = jnp.zeros((SUB, LANES), F32)
    for g in range(row_tiles + 1):
        for c, w in enumerate(coefficients(line * rows - 3 + g * SUB + tile_iota(0), extent)):
            xcoef[0, g, c] = w
    for r in range(row_tiles):
        for c, w in enumerate(coefficients(line * rows + r * SUB + tile_iota(0), extent)):
            xcoef[1, r, c] = w
    for var in range(4):
        for r in range(row_tiles + 2):
            prim[var, 0, r * SUB:(r + 1) * SUB, :] = zero
            prim[var, tiles + 1, r * SUB:(r + 1) * SUB, :] = zero
    for j in range(CHUNK):
        for r in range(row_tiles + 1):
            fx[j, 0, r * SUB:(r + 1) * SUB, :] = zero

    def body(step, carry):
        for j in range(CHUNK):
            t = step * CHUNK + j
            flux = []
            for rt in range(row_tiles):
                state = load_state(refs, rt, t)
                u, p, temp = primitive_of(state)
                at = slice((rt + 1) * SUB, (rt + 2) * SUB)
                for var, x in enumerate(u + [temp]):
                    prim[var, t + 1, at, :] = x
                press[t, rt * SUB:(rt + 1) * SUB, :] = p
                flux.append(convective(state, u, p, 0))
            for var in range(4):
                prim[var, t + 1, 0:SUB, :] = zero
                prim[var, t + 1, (row_tiles + 1) * SUB:(row_tiles + 2) * SUB, :] = zero
            for var in range(4):
                scale = -viscosity * (conduction if var == 3 else 1.0)
                for g in range(row_tiles + 1):
                    base = SUB - 3 + g * SUB
                    at = lambda k: prim[var, t + 1, base + k:base + k + SUB, :]
                    if 0 < g < row_tiles:
                        d = interior(at)
                    else:
                        d = apply([xcoef[0, g, c] for c in range(4)], at)
                    fx[j, var + 1, g * SUB:(g + 1) * SUB, :] = scale * d
            for rt in range(row_tiles):
                place = slice(3 + rt * SUB, 3 + (rt + 1) * SUB)
                for var, f in enumerate(flux[rt]):
                    fx[j, var, place, :] = fx[j, var, place, :] + f if var else f
            for var in range(5):
                for rt in range(row_tiles):
                    w = [xcoef[1, rt, c] for c in range(4)]
                    base = 3 + rt * SUB
                    xd_ref[var, t, rt * SUB:(rt + 1) * SUB, :] = apply(
                        w, lambda k: fx[j, var, base + k:base + k + SUB, :])
        return carry

    lax.fori_loop(0, tiles // CHUNK, body, 0)
    by_parity(0, lambda up: side_of(refs, up, near_ref, row_tiles - 1 if up else 0, 0, tiles))

    width = slot_width(row_tiles)
    per = LANES // width
    lane = tile_iota(1)

    def spread(ref, k):
        return jnp.broadcast_to(ref[0:1, k:k + 1], (SUB, LANES))

    count = spread(lists, 0) >> 16
    share = 1.0 / count.astype(F32)
    flipped = (lane % width) // row_tiles == 2
    for n in range(mix_ref.shape[0]):
        weight = zero
        for k in range(lists.shape[1]):
            turn = 1.0 - 2.0 * (spread(lists, k) & 1).astype(F32)
            hit = (lane // width + n * per == ((spread(lists, k) >> 1) & 0x7FFF)) & (k < count)
            weight = weight + jnp.where(hit, share * jnp.where(flipped, turn, 1.0), 0.0)
        mix_ref[n] = weight


def second_kernel(density, momentum, energy, prim, press, fy_ref, edge):
    refs = (density, momentum, energy)
    rows, cols = density.shape
    row_tiles, tiles = rows // SUB, cols // LANES
    zero = jnp.zeros((SUB, LANES), F32)
    lane_weights(edge, cols)
    for var in range(5):
        for r in range(row_tiles):
            fy_ref[var, 0, r * SUB:(r + 1) * SUB, :] = zero
            fy_ref[var, tiles + 1, r * SUB:(r + 1) * SUB, :] = zero

    def store(rt, t, grads):
        at = slice((rt + 1) * SUB, (rt + 2) * SUB)
        own = slice(rt * SUB, (rt + 1) * SUB)
        u = [prim[a, t + 1, at, :] for a in range(3)]
        for var, f in enumerate(convective(load_state(refs, rt, t), u, press[t, own, :], 1)):
            scale = viscosity * (conduction if var == 4 else 1.0)
            fy_ref[var, t + 1, own, :] = f - scale * grads[var - 1] if var else f

    def body(step, carry):
        t0 = step * WIDE
        weights = weights_at(edge, t0, tiles)
        for rt in range(row_tiles):
            at = slice((rt + 1) * SUB, (rt + 2) * SUB)
            grads = [lane_difference([prim[var, t0 + j, at, :] for j in range(WIDE + 2)], weights) for var in range(4)]
            for j in range(WIDE):
                store(rt, t0 + j, [g[j] for g in grads])
        return carry

    lax.fori_loop(0, tiles // WIDE, body, 0)


def volume_kernel(density, momentum, energy, adjoint, fy, xd, res_ref, sum_ref, edge):
    refs = (density, momentum, energy)
    rows, cols = density.shape
    row_tiles, tiles = rows // SUB, cols // LANES
    lane_weights(edge, cols)

    def body(step, accs):
        t0 = step * WIDE
        accs = list(accs)
        weights = weights_at(edge, t0, tiles)
        for rt in range(row_tiles):
            own = slice(rt * SUB, (rt + 1) * SUB)
            for var in range(5):
                dy = lane_difference([fy[var, t0 + j, own, :] for j in range(WIDE + 2)], weights)
                for j in range(WIDE):
                    t = t0 + j
                    r = xd[var, t, own, :] + dy[j]
                    res_ref[var, t, own, :] = r
                    weighted = adjoint[var, own, pl.ds(pl.multiple_of(t * LANES, LANES), LANES)] * r
                    accs[j % len(accs)] = accs[j % len(accs)] + weighted
        return tuple(accs)

    zero = jnp.zeros((SUB, LANES), F32)
    accs = lax.fori_loop(0, tiles // WIDE, body, (zero,) * 4)
    acc = (accs[0] + accs[1]) + (accs[2] + accs[3])
    weight = jnp.where(tile_iota(1) == LANES - 1, penalty, 0.0)
    last = tiles - 1
    for rt in range(row_tiles):
        own = slice(rt * SUB, (rt + 1) * SUB)
        for var, x in enumerate(load_state(refs, rt, last)):
            extra = weight * x
            res_ref[var, last, own, :] = res_ref[var, last, own, :] + extra
            acc = acc + adjoint[var, own, last * LANES:] * extra
    sum_ref[...] = acc


def border_kernel(chip, across, slots, mix, res, adjoint, total, out_ref, sum_ref, stage, sems):
    rows, cols = adjoint.shape[1:]
    row_tiles, tiles = rows // SUB, cols // LANES
    odd = lax.rem(lax.axis_index("line"), 2) == 1

    def body(t, acc):
        at = pl.ds(pl.multiple_of(t * LANES, LANES), LANES)
        near = [chip[n, :, at] for n in range(4)]
        far = [across[n, :, at] for n in range(4)]
        below = unpack([jnp.where(odd, a, b) for a, b in zip(near, far)], True)
        above = unpack([jnp.where(odd, b, a) for a, b in zip(near, far)], False)
        for var in range(5):
            for rt in range(row_tiles):
                own = slice(rt * SUB, (rt + 1) * SUB)
                r = res[var, t, own, :]
                for there, extra in ((0, below[var]), (row_tiles - 1, above[var])):
                    if rt == there:
                        r = r + extra
                        acc = acc + adjoint[var, own, at] * extra
                stage[var, own, at] = r
        return acc

    parts = 4
    size = tiles // parts
    copies = []
    acc = total[...]
    lane = tile_iota(1)
    for n in range(parts - 1, -1, -1):
        acc = lax.fori_loop(n * size, (n + 1) * size, body, acc, unroll=2)
        if n == parts - 1:
            target = slots[0] * mix[0]
            for m in range(1, slots.shape[0]):
                target = target + slots[m] * mix[m]
            step = slot_width(row_tiles)
            while step < LANES:
                target = target + pltpu.roll(target, step, 1)
                step *= 2
            for var in range(5):
                for rt in range(row_tiles):
                    own = slice(rt * SUB, (rt + 1) * SUB)
                    moved = pltpu.roll(target, LANES - 1 - (var * row_tiles + rt), 1)
                    extra = jnp.where(lane == LANES - 1, -penalty * moved, 0.0)
                    cut = slice((tiles - 1) * LANES, tiles * LANES)
                    stage[var, own, cut] = stage[var, own, cut] + extra
                    acc = acc + adjoint[var, own, cut] * extra
        cut = pl.ds(n * size * LANES, size * LANES)
        copies.append(pltpu.make_async_copy(stage.at[:, :, cut], out_ref.at[:, :, cut], sems.at[n]))
        copies[-1].start()
    points = rows * lax.axis_size("line") * cols
    sum_ref[...] = jnp.full((SUB, LANES), jnp.sum(acc) / points)
    for c in copies:
        c.wait()


def total_kernel(*refs):
    total = refs[0][...]
    for x in refs[1:-1]:
        total = total + x[...]
    refs[-1][0] = total[0, 0]


def per_device(density, momentum, energy, adjoint, partners, counts, orient):
    rows, cols = density.shape[1:]
    row_tiles, tiles = rows // SUB, cols // LANES
    lines, blocks = lax.axis_size("line"), lax.axis_size("blk")
    state = (density[0], momentum[0], energy[0])
    shape = jax.ShapeDtypeStruct
    pieces = -(-blocks * slot_width(row_tiles) // LANES)
    packed = shape((4, SUB, cols), F32)
    flat = shape((pieces, SUB, LANES), F32)
    anywhere = pl.BlockSpec(memory_space=pl.ANY)
    in_hbm = pl.BlockSpec(memory_space=pltpu.HBM)
    dma = pltpu.SemaphoreType.DMA

    def cost(micros):
        return pl.CostEstimate(flops=micros * 10**6, bytes_accessed=micros * 3 * 10**6, transcendentals=0)

    send_far, slots = pl.pallas_call(
        pack_kernel, out_shape=[packed, flat], in_specs=[in_hbm] * 3, out_specs=[whole()] * 2,
        scratch_shapes=[pltpu.VMEM((5, SUB, cols), F32), pltpu.VMEM((5, rows, LANES), F32), dma((3, 5))],
        compiler_params=params(), cost_estimate=cost(2),
    )(*[pltpu.with_memory_space_constraint(x, pltpu.HBM) for x in state])
    far = lax.ppermute(send_far, "line", [p for i in range(1, lines - 1, 2) for p in ((i, i + 1), (i + 1, i))])
    rounds = [slots]
    hop = 1
    while hop < blocks:
        got = lax.ppermute(rounds[-1], "blk", [(i, i ^ hop) for i in range(blocks)])
        rounds.append(rounds[-1] + got)
        hop *= 2
    slots = rounds[-1]

    lists = (counts[:, None] << 16) + (partners << 1) + orient
    prim, press, xd, send_near, mix = pl.pallas_call(
        first_kernel,
        out_shape=[shape((4, tiles + 2, rows + 2 * SUB, LANES), F32), shape((tiles, rows, LANES), F32),
                   shape((5, tiles, rows, LANES), F32), packed, flat],
        in_specs=[whole()] * 4, out_specs=[whole()] * 5,
        scratch_shapes=[
            pltpu.VMEM((CHUNK, 5, rows + SUB, LANES), F32),
            pltpu.VMEM((2, row_tiles + 1, 4, SUB, LANES), F32),
        ],
        compiler_params=params(), cost_estimate=cost(3),
    )(*state, lists)
    near = lax.ppermute(send_near, "line", [(i, i ^ 1) for i in range(lines)])
    fy = pl.pallas_call(
        second_kernel, out_shape=shape((5, tiles + 2, rows, LANES), F32),
        in_specs=[whole()] * 5, out_specs=whole(), scratch_shapes=[pltpu.VMEM((3, 6, SUB, LANES), F32)],
        compiler_params=params(), cost_estimate=cost(2),
    )(*state, prim, press)
    res, total = pl.pallas_call(
        volume_kernel,
        out_shape=[shape((5, tiles, rows, LANES), F32), shape((SUB, LANES), F32)],
        in_specs=[whole()] * 6, out_specs=[whole()] * 2,
        scratch_shapes=[pltpu.VMEM((3, 6, SUB, LANES), F32)], compiler_params=params(), cost_estimate=cost(2),
    )(*state, adjoint[0], fy, xd)
    result, part = pl.pallas_call(
        border_kernel,
        out_shape=[shape((5, rows, cols), F32), shape((SUB, LANES), F32)],
        in_specs=[whole()] * 7, out_specs=[anywhere, whole()],
        scratch_shapes=[pltpu.VMEM((5, rows, cols), F32), dma((4,))],
        compiler_params=params(), cost_estimate=cost(2),
    )(near, far, slots, mix, res, adjoint[0], total)
    if lines <= 4:
        parts = [part] + [lax.ppermute(part, "line", [(i, i ^ s) for i in range(lines)]) for s in range(1, lines)]
        correction = pl.pallas_call(
            total_kernel, out_shape=shape((1,), F32), in_specs=[whole()] * lines,
            out_specs=pl.BlockSpec(memory_space=pltpu.SMEM), compiler_params=params(),
        )(*parts)
    else:
        correction = lax.psum(part, "line")[0, 0:1]
    return result[None], correction


def solution(mesh):
    return jax.shard_map(
        per_device,
        mesh=mesh,
        in_specs=(
            P("blk", "line", None),
            P("blk", None, "line", None),
            P("blk", "line", None),
            P("blk", None, "line", None),
            P("blk", None),
            P("blk"),
            P("blk", None),
        ),
        out_specs=(P("blk", None, "line", None), P("blk")),
        check_vma=False,
    )
```

```python
import jax
import jax.numpy as jnp
import numpy as np
from jax import lax
from jax.experimental import pallas as pl
from jax.experimental.pallas import tpu as pltpu
from jax.sharding import PartitionSpec as P


STENCIL = (0.75, -0.15, 1.0 / 60.0)
gamma_less = 0.4
viscosity = 0.5
conduction = 1.5
penalty = 4.0
LANES = 128
SUB = 8
CHUNK = 4
WIDE = 16
PIECES = 3
F32 = jnp.float32
VMEM_LIMIT = 20 * 1024 * 1024

_ONE = {k: STENCIL[k - 1] for k in (1, 2, 3)}
_ONE.update({-k: -STENCIL[k - 1] for k in (1, 2, 3)})
TWICE = [sum(_ONE[a] * _ONE[b] for a in _ONE for b in _ONE if a + b == m) for m in range(7)]


def tile_iota(axis):
    return lax.broadcasted_iota(jnp.int32, (SUB, LANES), axis)


def coefficients(index, extent):
    inside = (index >= 0) & (index < extent)
    end = (index == 0) | (index == extent - 1)
    second = (index == 1) | (index == extent - 2)
    fourth = (index == 2) | (index == extent - 3)
    one = jnp.where(fourth, 2.0 / 3.0, jnp.where(second, 0.5, jnp.where(end, 1.0, STENCIL[0])))
    two = jnp.where(fourth, -1.0 / 12.0, jnp.where(second | end, 0.0, STENCIL[1]))
    three = jnp.where(fourth | second | end, 0.0, STENCIL[2])
    point = jnp.where(index == 0, -1.0, jnp.where(index == extent - 1, 1.0, 0.0))
    return [jnp.where(inside, c, 0.0).astype(F32) for c in (one, two, three, point)]


def load_state(refs, rt, t):
    density, momentum, energy = refs
    rows = slice(rt * SUB, (rt + 1) * SUB)
    cols = pl.ds(t * LANES if isinstance(t, int) else pl.multiple_of(t * LANES, LANES), LANES)
    return [density[rows, cols]] + [momentum[a, rows, cols] for a in range(3)] + [energy[rows, cols]]


def primitive_of(state):
    rho, m0, m1, m2, e = state
    inv = 1.0 / rho
    u = [m0 * inv, m1 * inv, m2 * inv]
    p = gamma_less * (e - 0.5 * (m0 * u[0] + m1 * u[1] + m2 * u[2]))
    return u, p, p * inv


def convective(state, u, p, d):
    n = u[d]
    out = [state[1 + d]]
    for a in range(3):
        f = state[1 + a] * n
        out.append(f + p if a == d else f)
    out.append((state[4] + p) * n)
    return out


def contribution(state, up):
    u, p, temp = primitive_of(state)
    conv = convective(state, u, p, 0)
    row = tile_iota(0)
    shift = (lambda x, m: pltpu.roll(x, m, 0)) if up else (lambda x, m: pltpu.roll(x, SUB - m, 0))
    sign = -1.0 if up else 1.0
    keep = [None] + [(row < m) if up else (row >= SUB - m) for m in range(1, 7)]
    out = []
    for var in range(5):
        acc = None
        for m in (1, 2, 3):
            term = shift(conv[var], m) * jnp.where(keep[m], sign * STENCIL[m - 1], 0.0)
            acc = term if acc is None else acc + term
        if var:
            prim = u[var - 1] if var < 4 else temp
            scale = -viscosity * (conduction if var == 4 else 1.0)
            for m in range(1, 7):
                acc = acc + shift(prim, m) * jnp.where(keep[m], scale * TWICE[m], 0.0)
        out.append(acc)
    mass, first, second = out[0], out[1], out[2]
    if up:
        first = jnp.where(row >= 6, pltpu.roll(mass, 6, 0), first)
        second = jnp.where(row == 6, pltpu.roll(mass, 4, 0), second)
    else:
        first = jnp.where(row < 2, pltpu.roll(mass, 3, 0), first)
        second = jnp.where(row == 0, pltpu.roll(mass, 1, 0), second)
    return [first, second, out[3], out[4]]


def unpack(tiles, up):
    row = tile_iota(0)
    first, second, third, fourth = tiles
    if up:
        mass = jnp.where(row < 2, pltpu.roll(first, 2, 0), 0.0) + jnp.where(row == 2, pltpu.roll(second, 4, 0), 0.0)
        keep = row < 6
    else:
        mass = jnp.where((row == 5) | (row == 6), pltpu.roll(first, 5, 0), 0.0) + jnp.where(
            row == 7, pltpu.roll(second, 7, 0), 0.0)
        keep = row >= 2
    return [mass] + [jnp.where(keep, x, 0.0) for x in (first, second, third, fourth)]


def side_of(refs, up, out_ref, rt, first, last):
    def body(t, carry):
        cols = pl.ds(pl.multiple_of(t * LANES, LANES), LANES)
        for n, x in enumerate(contribution(load_state(refs, rt, t), up)):
            out_ref[n, :, cols] = x
        return carry

    lax.fori_loop(first, last, body, 0, unroll=2)


def by_parity(up_when, run):
    odd = lax.rem(lax.axis_index("line"), 2)

    @pl.when(odd == up_when)
    def _():
        run(True)

    @pl.when(odd != up_when)
    def _():
        run(False)


def pack_kernel(density, momentum, energy, out_ref, slots, buf, other, sems):
    rows, cols = density.shape
    row_tiles, tiles = rows // SUB, cols // LANES
    up = lax.rem(lax.axis_index("line"), 2) == 1
    mine = jnp.where(up, row_tiles - 1, 0)
    sources = [density] + [momentum.at[a] for a in range(3)] + [energy]
    halves = 2
    part = cols // halves
    copies = []
    for h in range(halves):
        for n, x in enumerate(sources):
            at = pl.ds(pl.multiple_of(mine * SUB, SUB), SUB)
            copies.append(pltpu.make_async_copy(
                x.at[at, pl.ds(h * part, part)], buf.at[n, :, pl.ds(h * part, part)], sems.at[h, n]))
    bottom = [pltpu.make_async_copy(x.at[:, pl.ds(0, LANES)], other.at[n], sems.at[halves, n])
              for n, x in enumerate(sources)]
    for c in copies + bottom:
        c.start()

    refs = (buf.at[0], buf.at[1:4], buf.at[4])
    for h in range(halves):
        for c in copies[h * 5:(h + 1) * 5]:
            c.wait()
        by_parity(1, lambda up_side: side_of(refs, up_side, out_ref, 0, h * tiles // halves, (h + 1) * tiles // halves))

    for c in bottom:
        c.wait()
    width = slot_width(row_tiles)
    per = LANES // width
    block = lax.axis_index("blk")
    lane = tile_iota(1)
    base = lax.rem(block, per) * width
    value = jnp.zeros((SUB, LANES), F32)
    for rt in range(row_tiles):
        for var in range(5):
            x = other[var, rt * SUB:(rt + 1) * SUB, 0:1]
            value = jnp.where(lane == base + (var * row_tiles + rt), x, value)
    for n in range(slots.shape[0]):
        slots[n] = jnp.where(block // per == n, value, 0.0)


def slot_width(row_tiles):
    width = 1
    while width < 5 * row_tiles:
        width *= 2
    return width


def whole():
    return pl.BlockSpec(memory_space=pltpu.VMEM)


def params():
    return pltpu.CompilerParams(vmem_limit_bytes=VMEM_LIMIT)


def line_operator(cols):
    out = np.zeros((3, 2 * LANES, LANES), np.float32)
    for n, start in enumerate((0, LANES, cols - LANES)):
        for lane in range(LANES):
            at = start + lane
            edge = min(at, cols - 1 - at)
            if edge == 0:
                terms = {0: -60, 1: 60} if at == 0 else {0: 60, -1: -60}
            else:
                half = {1: (30,), 2: (40, -5)}.get(edge, (45, -9, 1))
                terms = {sign * (k + 1): sign * c for k, c in enumerate(half) for sign in (1, -1)}
            for offset, c in terms.items():
                out[n, (lane + offset) % (2 * LANES), lane] = c
    return np.tile(out, (1, PIECES, 1)).astype(jnp.bfloat16)


def split(x):
    pieces = []
    for _ in range(PIECES):
        piece = x.astype(jnp.bfloat16)
        pieces.append(piece)
        x = x - piece.astype(F32)
    return pieces


def wide_of(tiles):
    return max(w for w in range(1, WIDE + 1) if tiles % w == 0 and 2 * w <= tiles)


def lane_differences(lhs, operator, tile_of, wide, count, step, last):
    rows = lhs.shape[0] // (wide * count)
    lane = lax.broadcasted_iota(jnp.int32, (rows, LANES), 1)
    for var in range(count):
        for j in range(wide):
            at = slice((j * count + var) * rows, (j * count + var + 1) * rows)
            cur = split(tile_of(var, j))
            mix = split(jnp.where(lane < LANES // 2, tile_of(var, j + 1), tile_of(var, j - 1)))
            for n in range(PIECES):
                lhs[at, 2 * n * LANES:(2 * n + 1) * LANES] = cur[n]
                lhs[at, (2 * n + 1) * LANES:(2 * n + 2) * LANES] = mix[n]
    out = jnp.dot(lhs[...], operator[1], preferred_element_type=F32)
    which = jnp.where(step == 0, 0, jnp.where(step == last, 2, 1))
    size = count * rows
    start = pl.multiple_of(jnp.where(step == last, (wide - 1) * size, 0), size)
    end = jnp.dot(lhs[pl.ds(start, size), :], operator[which], preferred_element_type=F32)
    return (lambda var, j: out[(j * count + var) * rows:(j * count + var + 1) * rows],
            lambda var: end[var * rows:(var + 1) * rows])


def apply(weights, at):
    one, two, three, point = weights
    return one * (at(1) - at(-1)) + two * (at(2) - at(-2)) + three * (at(3) - at(-3)) + point * at(0)


def interior(at):
    one, two, three = STENCIL
    return one * (at(1) - at(-1)) + two * (at(2) - at(-2)) + three * (at(3) - at(-3))


def first_kernel(density, momentum, energy, lists,
                 prim, press, xd_ref, near_ref, mix_ref, fx, xcoef):
    refs = (density, momentum, energy)
    rows, cols = density.shape
    row_tiles, tiles = rows // SUB, cols // LANES
    line = lax.axis_index("line")
    extent = rows * lax.axis_size("line")
    zero = jnp.zeros((SUB, LANES), F32)
    for g in range(row_tiles + 1):
        for c, w in enumerate(coefficients(line * rows - 3 + g * SUB + tile_iota(0), extent)):
            xcoef[0, g, c] = w
    for r in range(row_tiles):
        for c, w in enumerate(coefficients(line * rows + r * SUB + tile_iota(0), extent)):
            xcoef[1, r, c] = w
    for var in range(4):
        for r in range(row_tiles + 2):
            prim[var, 0, r * SUB:(r + 1) * SUB, :] = zero
            prim[var, tiles + 1, r * SUB:(r + 1) * SUB, :] = zero
    for j in range(CHUNK):
        for r in range(row_tiles + 1):
            fx[j, 0, r * SUB:(r + 1) * SUB, :] = zero

    def body(step, carry):
        for j in range(CHUNK):
            t = step * CHUNK + j
            flux = []
            for rt in range(row_tiles):
                state = load_state(refs, rt, t)
                u, p, temp = primitive_of(state)
                at = slice((rt + 1) * SUB, (rt + 2) * SUB)
                for var, x in enumerate(u + [temp]):
                    prim[var, t + 1, at, :] = x
                press[t, rt * SUB:(rt + 1) * SUB, :] = p
                flux.append(convective(state, u, p, 0))
            for var in range(4):
                prim[var, t + 1, 0:SUB, :] = zero
                prim[var, t + 1, (row_tiles + 1) * SUB:(row_tiles + 2) * SUB, :] = zero
            for var in range(4):
                scale = -viscosity * (conduction if var == 3 else 1.0)
                for g in range(row_tiles + 1):
                    base = SUB - 3 + g * SUB
                    at = lambda k: prim[var, t + 1, base + k:base + k + SUB, :]
                    if 0 < g < row_tiles:
                        d = interior(at)
                    else:
                        d = apply([xcoef[0, g, c] for c in range(4)], at)
                    fx[j, var + 1, g * SUB:(g + 1) * SUB, :] = scale * d
            for rt in range(row_tiles):
                place = slice(3 + rt * SUB, 3 + (rt + 1) * SUB)
                for var, f in enumerate(flux[rt]):
                    fx[j, var, place, :] = fx[j, var, place, :] + f if var else f
            for var in range(5):
                for rt in range(row_tiles):
                    w = [xcoef[1, rt, c] for c in range(4)]
                    base = 3 + rt * SUB
                    xd_ref[var, t, rt * SUB:(rt + 1) * SUB, :] = apply(
                        w, lambda k: fx[j, var, base + k:base + k + SUB, :])
        return carry

    lax.fori_loop(0, tiles // CHUNK, body, 0)
    by_parity(0, lambda up: side_of(refs, up, near_ref, row_tiles - 1 if up else 0, 0, tiles))

    width = slot_width(row_tiles)
    per = LANES // width
    lane = tile_iota(1)

    def spread(ref, k):
        return jnp.broadcast_to(ref[0:1, k:k + 1], (SUB, LANES))

    count = spread(lists, 0) >> 16
    share = 1.0 / count.astype(F32)
    flipped = (lane % width) // row_tiles == 2
    for n in range(mix_ref.shape[0]):
        weight = zero
        for k in range(lists.shape[1]):
            turn = 1.0 - 2.0 * (spread(lists, k) & 1).astype(F32)
            hit = (lane // width + n * per == ((spread(lists, k) >> 1) & 0x7FFF)) & (k < count)
            weight = weight + jnp.where(hit, share * jnp.where(flipped, turn, 1.0), 0.0)
        mix_ref[n] = weight


def second_kernel(density, momentum, energy, prim, press, operator, fy_ref, lhs):
    rows, cols = density.shape
    tiles = cols // LANES
    wide = wide_of(tiles)
    last = tiles // wide - 1
    zero = jnp.zeros((rows, LANES), F32)
    for var in range(5):
        fy_ref[var, 0] = zero
        fy_ref[var, tiles + 1] = zero
    own = slice(SUB, SUB + rows)

    def store(t, grads):
        cut = pl.ds(pl.multiple_of(t * LANES, LANES), LANES)
        state = [density[:, cut]] + [momentum[a, :, cut] for a in range(3)] + [energy[:, cut]]
        u = [prim[a, t + 1, own, :] for a in range(3)]
        for var, f in enumerate(convective(state, u, press[t], 1)):
            scale = viscosity * (conduction if var == 4 else 1.0) / 60.0
            fy_ref[var, t + 1] = f - scale * grads(var - 1) if var else f

    def body(step, carry):
        t0 = step * wide
        inner, end = lane_differences(
            lhs, operator, lambda var, j: prim[var, t0 + j + 1, own, :], wide, 4, step, last)
        for j in range(wide):
            store(t0 + j, lambda var: inner(var, j))
        store(jnp.where(step == last, tiles - 1, t0), end)
        return carry

    lax.fori_loop(0, last + 1, body, 0)


def volume_kernel(density, momentum, energy, adjoint, fy, xd, operator, res_ref, sum_ref, lhs):
    refs = (density, momentum, energy)
    rows, cols = density.shape
    row_tiles, tiles = rows // SUB, cols // LANES
    wide = wide_of(tiles)
    last = tiles // wide - 1

    def body(step, accs):
        t0 = step * wide
        accs = list(accs)
        inner, end = lane_differences(lhs, operator, lambda var, j: fy[var, t0 + j + 1], wide, 5, step, last)
        at_end = jnp.where(step == last, tiles - 1, t0)
        for var in range(5):
            for j in range(wide):
                t = t0 + j
                r = xd[var, t] + inner(var, j) * (1.0 / 60.0)
                res_ref[var, t] = r
                accs[j % 2] = accs[j % 2] + adjoint[var, :, pl.ds(pl.multiple_of(t * LANES, LANES), LANES)] * r
        for var in range(5):
            r = xd[var, at_end] + end(var) * (1.0 / 60.0)
            change = r - res_ref[var, at_end]
            res_ref[var, at_end] = r
            accs[var % 2] = accs[var % 2] + adjoint[var, :, pl.ds(pl.multiple_of(at_end * LANES, LANES), LANES)] * change
        return tuple(accs)

    zero = jnp.zeros((rows, LANES), F32)
    one, two = lax.fori_loop(0, last + 1, body, (zero, zero))
    both = one + two
    acc = both[0:SUB]
    for rt in range(1, row_tiles):
        acc = acc + both[rt * SUB:(rt + 1) * SUB]
    weight = jnp.where(tile_iota(1) == LANES - 1, penalty, 0.0)
    for rt in range(row_tiles):
        own = slice(rt * SUB, (rt + 1) * SUB)
        for var, x in enumerate(load_state(refs, rt, tiles - 1)):
            extra = weight * x
            res_ref[var, tiles - 1, own, :] = res_ref[var, tiles - 1, own, :] + extra
            acc = acc + adjoint[var, own, (tiles - 1) * LANES:] * extra
    sum_ref[...] = acc


def border_kernel(chip, across, slots, mix, res, adjoint, total, out_ref, sum_ref, stage, sems):
    rows, cols = adjoint.shape[1:]
    row_tiles, tiles = rows // SUB, cols // LANES
    odd = lax.rem(lax.axis_index("line"), 2) == 1

    def body(t, acc):
        at = pl.ds(pl.multiple_of(t * LANES, LANES), LANES)
        near = [chip[n, :, at] for n in range(4)]
        far = [across[n, :, at] for n in range(4)]
        below = unpack([jnp.where(odd, a, b) for a, b in zip(near, far)], True)
        above = unpack([jnp.where(odd, b, a) for a, b in zip(near, far)], False)
        for var in range(5):
            for rt in range(row_tiles):
                own = slice(rt * SUB, (rt + 1) * SUB)
                r = res[var, t, own, :]
                for there, extra in ((0, below[var]), (row_tiles - 1, above[var])):
                    if rt == there:
                        r = r + extra
                        acc = acc + adjoint[var, own, at] * extra
                stage[var, own, at] = r
        return acc

    parts = 4
    size = tiles // parts
    copies = []
    acc = total[...]
    lane = tile_iota(1)
    for n in range(parts - 1, -1, -1):
        acc = lax.fori_loop(n * size, (n + 1) * size, body, acc, unroll=2)
        if n == parts - 1:
            target = slots[0] * mix[0]
            for m in range(1, slots.shape[0]):
                target = target + slots[m] * mix[m]
            step = slot_width(row_tiles)
            while step < LANES:
                target = target + pltpu.roll(target, step, 1)
                step *= 2
            for var in range(5):
                for rt in range(row_tiles):
                    own = slice(rt * SUB, (rt + 1) * SUB)
                    moved = pltpu.roll(target, LANES - 1 - (var * row_tiles + rt), 1)
                    extra = jnp.where(lane == LANES - 1, -penalty * moved, 0.0)
                    cut = slice((tiles - 1) * LANES, tiles * LANES)
                    stage[var, own, cut] = stage[var, own, cut] + extra
                    acc = acc + adjoint[var, own, cut] * extra
        cut = pl.ds(n * size * LANES, size * LANES)
        copies.append(pltpu.make_async_copy(stage.at[:, :, cut], out_ref.at[:, :, cut], sems.at[n]))
        copies[-1].start()
    points = rows * lax.axis_size("line") * cols
    sum_ref[...] = jnp.full((SUB, LANES), jnp.sum(acc) / points)
    for c in copies:
        c.wait()


def total_kernel(*refs):
    total = refs[0][...]
    for x in refs[1:-1]:
        total = total + x[...]
    refs[-1][0] = total[0, 0]


def per_device(density, momentum, energy, adjoint, partners, counts, orient):
    rows, cols = density.shape[1:]
    row_tiles, tiles = rows // SUB, cols // LANES
    lines, blocks = lax.axis_size("line"), lax.axis_size("blk")
    state = (density[0], momentum[0], energy[0])
    shape = jax.ShapeDtypeStruct
    pieces = -(-blocks * slot_width(row_tiles) // LANES)
    packed = shape((4, SUB, cols), F32)
    flat = shape((pieces, SUB, LANES), F32)
    anywhere = pl.BlockSpec(memory_space=pl.ANY)
    in_hbm = pl.BlockSpec(memory_space=pltpu.HBM)
    dma = pltpu.SemaphoreType.DMA

    def cost(micros):
        return pl.CostEstimate(flops=micros * 10**6, bytes_accessed=micros * 3 * 10**6, transcendentals=0)

    send_far, slots = pl.pallas_call(
        pack_kernel, out_shape=[packed, flat], in_specs=[in_hbm] * 3, out_specs=[whole()] * 2,
        scratch_shapes=[pltpu.VMEM((5, SUB, cols), F32), pltpu.VMEM((5, rows, LANES), F32), dma((3, 5))],
        compiler_params=params(), cost_estimate=cost(2),
    )(*[pltpu.with_memory_space_constraint(x, pltpu.HBM) for x in state])
    far = lax.ppermute(send_far, "line", [p for i in range(1, lines - 1, 2) for p in ((i, i + 1), (i + 1, i))])
    rounds = [slots]
    hop = 1
    while hop < blocks:
        got = lax.ppermute(rounds[-1], "blk", [(i, i ^ hop) for i in range(blocks)])
        rounds.append(rounds[-1] + got)
        hop *= 2
    slots = rounds[-1]

    operator = jnp.asarray(line_operator(cols))

    def lhs_of(count):
        return pltpu.VMEM((wide_of(tiles) * count * rows, 2 * PIECES * LANES), jnp.bfloat16)

    lists = (counts[:, None] << 16) + (partners << 1) + orient
    prim, press, xd, send_near, mix = pl.pallas_call(
        first_kernel,
        out_shape=[shape((4, tiles + 2, rows + 2 * SUB, LANES), F32), shape((tiles, rows, LANES), F32),
                   shape((5, tiles, rows, LANES), F32), packed, flat],
        in_specs=[whole()] * 4, out_specs=[whole()] * 5,
        scratch_shapes=[
            pltpu.VMEM((CHUNK, 5, rows + SUB, LANES), F32),
            pltpu.VMEM((2, row_tiles + 1, 4, SUB, LANES), F32),
        ],
        compiler_params=params(), cost_estimate=cost(3),
    )(*state, lists)
    near = lax.ppermute(send_near, "line", [(i, i ^ 1) for i in range(lines)])
    fy = pl.pallas_call(
        second_kernel, out_shape=shape((5, tiles + 2, rows, LANES), F32),
        in_specs=[whole()] * 6, out_specs=whole(), scratch_shapes=[lhs_of(4)],
        compiler_params=params(), cost_estimate=cost(2),
    )(*state, prim, press, operator)
    res, total = pl.pallas_call(
        volume_kernel,
        out_shape=[shape((5, tiles, rows, LANES), F32), shape((SUB, LANES), F32)],
        in_specs=[whole()] * 7, out_specs=[whole()] * 2,
        scratch_shapes=[lhs_of(5)], compiler_params=params(), cost_estimate=cost(2),
    )(*state, adjoint[0], fy, xd, operator)
    result, part = pl.pallas_call(
        border_kernel,
        out_shape=[shape((5, rows, cols), F32), shape((SUB, LANES), F32)],
        in_specs=[whole()] * 7, out_specs=[anywhere, whole()],
        scratch_shapes=[pltpu.VMEM((5, rows, cols), F32), dma((4,))],
        compiler_params=params(), cost_estimate=cost(2),
    )(near, far, slots, mix, res, adjoint[0], total)
    if lines <= 4:
        parts = [part] + [lax.ppermute(part, "line", [(i, i ^ s) for i in range(lines)]) for s in range(1, lines)]
        correction = pl.pallas_call(
            total_kernel, out_shape=shape((1,), F32), in_specs=[whole()] * lines,
            out_specs=pl.BlockSpec(memory_space=pltpu.SMEM), compiler_params=params(),
        )(*parts)
    else:
        correction = lax.psum(part, "line")[0, 0:1]
    return result[None], correction


def solution(mesh):
    return jax.shard_map(
        per_device,
        mesh=mesh,
        in_specs=(
            P("blk", "line", None),
            P("blk", None, "line", None),
            P("blk", "line", None),
            P("blk", None, "line", None),
            P("blk", None),
            P("blk"),
            P("blk", None),
        ),
        out_specs=(P("blk", None, "line", None), P("blk")),
        check_vma=False,
    )
```

```python
import jax
import jax.numpy as jnp
import numpy as np
from jax import lax
from jax.experimental import pallas as pl
from jax.experimental.pallas import tpu as pltpu
from jax.sharding import PartitionSpec as P


STENCIL = (0.75, -0.15, 1.0 / 60.0)
gamma_less = 0.4
viscosity = 0.5
conduction = 1.5
penalty = 4.0
LANES = 128
SUB = 8
CHUNK = 4
WIDE = 16
PIECES = 3
F32 = jnp.float32
VMEM_LIMIT = 20 * 1024 * 1024

_ONE = {k: STENCIL[k - 1] for k in (1, 2, 3)}
_ONE.update({-k: -STENCIL[k - 1] for k in (1, 2, 3)})
TWICE = [sum(_ONE[a] * _ONE[b] for a in _ONE for b in _ONE if a + b == m) for m in range(7)]


def tile_iota(axis):
    return lax.broadcasted_iota(jnp.int32, (SUB, LANES), axis)


def coefficients(index, extent):
    inside = (index >= 0) & (index < extent)
    end = (index == 0) | (index == extent - 1)
    second = (index == 1) | (index == extent - 2)
    fourth = (index == 2) | (index == extent - 3)
    one = jnp.where(fourth, 2.0 / 3.0, jnp.where(second, 0.5, jnp.where(end, 1.0, STENCIL[0])))
    two = jnp.where(fourth, -1.0 / 12.0, jnp.where(second | end, 0.0, STENCIL[1]))
    three = jnp.where(fourth | second | end, 0.0, STENCIL[2])
    point = jnp.where(index == 0, -1.0, jnp.where(index == extent - 1, 1.0, 0.0))
    return [jnp.where(inside, c, 0.0).astype(F32) for c in (one, two, three, point)]


def parts_of(state):
    return state.at[0], state.at[1:4], state.at[4]


def load_state(refs, rt, t):
    density, momentum, energy = refs
    rows = slice(rt * SUB, (rt + 1) * SUB)
    cols = pl.ds(t * LANES if isinstance(t, int) else pl.multiple_of(t * LANES, LANES), LANES)
    return [density[rows, cols]] + [momentum[a, rows, cols] for a in range(3)] + [energy[rows, cols]]


def primitive_of(state):
    rho, m0, m1, m2, e = state
    inv = 1.0 / rho
    u = [m0 * inv, m1 * inv, m2 * inv]
    p = gamma_less * (e - 0.5 * (m0 * u[0] + m1 * u[1] + m2 * u[2]))
    return u, p, p * inv


def convective(state, u, p, d):
    n = u[d]
    out = [state[1 + d]]
    for a in range(3):
        f = state[1 + a] * n
        out.append(f + p if a == d else f)
    out.append((state[4] + p) * n)
    return out


def contribution(state, up, pad):
    u, p, temp = primitive_of(state)
    conv = convective(state, u, p, 0)
    middle = slice(SUB, 2 * SUB)
    for n, x in enumerate(conv + u + [temp]):
        pad[n, middle, :] = x
    sign = -1.0 if up else 1.0

    def shifted(n, m):
        start = 2 * SUB - m if up else m
        return pad[n, start:start + SUB, :]

    out = []
    for var in range(5):
        acc = None
        for m in (1, 2, 3):
            term = shifted(var, m) * (sign * STENCIL[m - 1])
            acc = term if acc is None else acc + term
        if var:
            scale = -viscosity * (conduction if var == 4 else 1.0)
            for m in range(1, 7):
                acc = acc + shifted(4 + var, m) * (scale * TWICE[m])
        out.append(acc)
    return place_mass(out, up)


def place_mass(out, up):
    row = tile_iota(0)
    mass, first, second = out[0], out[1], out[2]
    if up:
        first = jnp.where(row >= 6, pltpu.roll(mass, 6, 0), first)
        second = jnp.where(row == 6, pltpu.roll(mass, 4, 0), second)
    else:
        first = jnp.where(row < 2, pltpu.roll(mass, 3, 0), first)
        second = jnp.where(row == 0, pltpu.roll(mass, 1, 0), second)
    return [first, second, out[3], out[4]]


def unpack(tiles, up):
    row = tile_iota(0)
    first, second, third, fourth = tiles
    if up:
        mass = jnp.where(row < 2, pltpu.roll(first, 2, 0), 0.0) + jnp.where(row == 2, pltpu.roll(second, 4, 0), 0.0)
        keep = row < 6
    else:
        mass = jnp.where((row == 5) | (row == 6), pltpu.roll(first, 5, 0), 0.0) + jnp.where(
            row == 7, pltpu.roll(second, 7, 0), 0.0)
        keep = row >= 2
    return [mass] + [jnp.where(keep, x, 0.0) for x in (first, second, third, fourth)]


def side_of(refs, up, out_ref, rt, first, last, pad):
    ways = pad.shape[0]

    def body(step, carry):
        for j in range(ways):
            t = step * ways + j
            cols = pl.ds(pl.multiple_of(t * LANES, LANES), LANES)
            for n, x in enumerate(contribution(load_state(refs, rt, t), up, pad.at[j])):
                out_ref[n, :, cols] = x
        return carry

    lax.fori_loop(first // ways, last // ways, body, 0)


def clear(pad):
    zero = jnp.zeros((SUB, LANES), F32)
    for j in range(pad.shape[0]):
        for n in range(pad.shape[1]):
            pad[j, n, 0:SUB, :] = zero
            pad[j, n, 2 * SUB:3 * SUB, :] = zero


def by_parity(up_when, run):
    odd = lax.rem(lax.axis_index("line"), 2)

    @pl.when(odd == up_when)
    def _():
        run(True)

    @pl.when(odd != up_when)
    def _():
        run(False)


def pack_kernel(density, momentum, energy, out_ref, slots, state_ref, pad, sems):
    rows, cols = density.shape
    row_tiles, tiles = rows // SUB, cols // LANES
    up = lax.rem(lax.axis_index("line"), 2) == 1
    mine = jnp.where(up, row_tiles - 1, 0)
    sources = [density] + [momentum.at[a] for a in range(3)] + [energy]
    halves = 2
    part = cols // halves

    def fetch(x, n, tile, h, sem):
        at = pl.ds(pl.multiple_of(tile * SUB, SUB), SUB)
        cut = pl.ds(h * part, part)
        return pltpu.make_async_copy(x.at[at, cut], state_ref.at[n, at, cut], sem)

    needed = [[fetch(x, n, mine, h, sems.at[h, n]) for n, x in enumerate(sources)] for h in range(halves)]
    rest = [fetch(x, n, jnp.where(mine == 0, k, k - 1), h, sems.at[halves * k + h, n])
            for k in range(1, row_tiles) for h in range(halves) for n, x in enumerate(sources)]
    for c in sum(needed, []) + rest:
        c.start()
    clear(pad)
    refs = parts_of(state_ref)
    for h in range(halves):
        for c in needed[h]:
            c.wait()
        by_parity(1, lambda up_side: side_of(
            refs, up_side, out_ref, row_tiles - 1 if up_side else 0, h * tiles // halves, (h + 1) * tiles // halves, pad))
    for c in rest:
        c.wait()
    width = slot_width(row_tiles)
    per = LANES // width
    block = lax.axis_index("blk")
    lane = tile_iota(1)
    base = lax.rem(block, per) * width
    value = jnp.zeros((SUB, LANES), F32)
    for rt in range(row_tiles):
        for var in range(5):
            x = state_ref[var, rt * SUB:(rt + 1) * SUB, 0:LANES][:, 0:1]
            value = jnp.where(lane == base + (var * row_tiles + rt), x, value)
    for n in range(slots.shape[0]):
        slots[n] = jnp.where(block // per == n, value, 0.0)


def slot_width(row_tiles):
    width = 1
    while width < 5 * row_tiles:
        width *= 2
    return width


def whole():
    return pl.BlockSpec(memory_space=pltpu.VMEM)


def params():
    return pltpu.CompilerParams(vmem_limit_bytes=VMEM_LIMIT)


def line_operator(cols):
    out = np.zeros((3, 2 * LANES, LANES), np.float32)
    for n, start in enumerate((0, LANES, cols - LANES)):
        for lane in range(LANES):
            at = start + lane
            edge = min(at, cols - 1 - at)
            if edge == 0:
                terms = {0: -60, 1: 60} if at == 0 else {0: 60, -1: -60}
            else:
                half = {1: (30,), 2: (40, -5)}.get(edge, (45, -9, 1))
                terms = {sign * (k + 1): sign * c for k, c in enumerate(half) for sign in (1, -1)}
            for offset, c in terms.items():
                out[n, (lane + offset) % (2 * LANES), lane] = c
    return np.tile(out, (1, PIECES, 1)).astype(jnp.bfloat16)


def split(x):
    pieces = []
    for _ in range(PIECES):
        piece = x.astype(jnp.bfloat16)
        pieces.append(piece)
        x = x - piece.astype(F32)
    return pieces


def wide_of(tiles):
    return max(w for w in range(1, WIDE + 1) if tiles % w == 0 and 2 * w <= tiles)


def lane_differences(lhs, operator, tile_of, wide, count, step, last):
    rows = lhs.shape[0] // (wide * count)
    lane = lax.broadcasted_iota(jnp.int32, (rows, LANES), 1)
    for var in range(count):
        for j in range(wide):
            at = slice((j * count + var) * rows, (j * count + var + 1) * rows)
            cur = split(tile_of(var, j))
            mix = split(jnp.where(lane < LANES // 2, tile_of(var, j + 1), tile_of(var, j - 1)))
            for n in range(PIECES):
                lhs[at, 2 * n * LANES:(2 * n + 1) * LANES] = cur[n]
                lhs[at, (2 * n + 1) * LANES:(2 * n + 2) * LANES] = mix[n]
    out = jnp.dot(lhs[...], operator[1], preferred_element_type=F32)
    which = jnp.where(step == 0, 0, jnp.where(step == last, 2, 1))
    size = count * rows
    start = pl.multiple_of(jnp.where(step == last, (wide - 1) * size, 0), size)
    end = jnp.dot(lhs[pl.ds(start, size), :], operator[which], preferred_element_type=F32)
    return (lambda var, j: out[(j * count + var) * rows:(j * count + var + 1) * rows],
            lambda var: end[var * rows:(var + 1) * rows])


def apply(weights, at):
    one, two, three, point = weights
    return one * (at(1) - at(-1)) + two * (at(2) - at(-2)) + three * (at(3) - at(-3)) + point * at(0)


def interior(at):
    one, two, three = STENCIL
    return one * (at(1) - at(-1)) + two * (at(2) - at(-2)) + three * (at(3) - at(-3))


def first_kernel(state_ref, counts, partners, orient,
                 prim, press, xd_ref, near_ref, mix_ref, fx, xcoef):
    refs = parts_of(state_ref)
    rows, cols = state_ref.shape[1:]
    row_tiles, tiles = rows // SUB, cols // LANES
    line = lax.axis_index("line")
    extent = rows * lax.axis_size("line")
    zero = jnp.zeros((SUB, LANES), F32)
    for g in range(row_tiles + 1):
        for c, w in enumerate(coefficients(line * rows - 3 + g * SUB + tile_iota(0), extent)):
            xcoef[0, g, c] = w
    for r in range(row_tiles):
        for c, w in enumerate(coefficients(line * rows + r * SUB + tile_iota(0), extent)):
            xcoef[1, r, c] = w
    for var in range(4):
        for r in range(row_tiles + 2):
            prim[var, 0, r * SUB:(r + 1) * SUB, :] = zero
            prim[var, tiles + 1, r * SUB:(r + 1) * SUB, :] = zero
    for j in range(CHUNK):
        for var in range(5):
            for r in range(row_tiles + 3):
                fx[j, var, r * SUB:(r + 1) * SUB, :] = zero
    odd = lax.rem(line, 2)
    beyond = pl.multiple_of((rows + SUB) * (1 - odd), SUB)

    def body(step, carry):
        for j in range(CHUNK):
            t = step * CHUNK + j
            flux = []
            for rt in range(row_tiles):
                state = load_state(refs, rt, t)
                u, p, temp = primitive_of(state)
                at = slice((rt + 1) * SUB, (rt + 2) * SUB)
                for var, x in enumerate(u + [temp]):
                    prim[var, t + 1, at, :] = x
                press[t, rt * SUB:(rt + 1) * SUB, :] = p
                flux.append(convective(state, u, p, 0))
            for var in range(4):
                prim[var, t + 1, 0:SUB, :] = zero
                prim[var, t + 1, (row_tiles + 1) * SUB:(row_tiles + 2) * SUB, :] = zero
            for var in range(4):
                scale = -viscosity * (conduction if var == 3 else 1.0)
                for g in range(row_tiles + 1):
                    base = SUB - 3 + g * SUB
                    at = lambda k: prim[var, t + 1, base + k:base + k + SUB, :]
                    if 0 < g < row_tiles:
                        d = interior(at)
                    else:
                        d = apply([xcoef[0, g, c] for c in range(4)], at)
                    fx[j, var + 1, (g + 1) * SUB:(g + 2) * SUB, :] = scale * d
            for rt in range(row_tiles):
                place = slice(11 + rt * SUB, 11 + (rt + 1) * SUB)
                for var, f in enumerate(flux[rt]):
                    fx[j, var, place, :] = fx[j, var, place, :] + f if var else f
            for var in range(5):
                for rt in range(row_tiles):
                    w = [xcoef[1, rt, c] for c in range(4)]
                    base = 11 + rt * SUB
                    xd_ref[var, t, rt * SUB:(rt + 1) * SUB, :] = apply(
                        w, lambda k: fx[j, var, base + k:base + k + SUB, :])
            out = [interior(lambda k: fx[j, var, pl.ds(beyond + (3 + k), SUB), :]) for var in range(5)]
            cut = pl.ds(pl.multiple_of(t * LANES, LANES), LANES)
            for n, (a, b) in enumerate(zip(place_mass(out, True), place_mass(out, False))):
                near_ref[n, :, cut] = jnp.where(odd == 1, b, a) if n < 2 else a
        return carry

    lax.fori_loop(0, tiles // CHUNK, body, 0)

    width = slot_width(row_tiles)
    per = LANES // width
    lane = tile_iota(1)

    def spread(ref, k):
        return jnp.broadcast_to(ref[0:1, k:k + 1], (SUB, LANES))

    count = spread(counts, 0)
    share = 1.0 / count.astype(F32)
    flipped = (lane % width) // row_tiles == 2
    for n in range(mix_ref.shape[0]):
        weight = zero
        for k in range(partners.shape[1]):
            turn = 1.0 - 2.0 * spread(orient, k).astype(F32)
            hit = (lane // width + n * per == spread(partners, k)) & (k < count)
            weight = weight + jnp.where(hit, share * jnp.where(flipped, turn, 1.0), 0.0)
        mix_ref[n] = weight


def second_kernel(state_ref, prim, press, operator, fy_ref, lhs):
    rows, cols = state_ref.shape[1:]
    tiles = cols // LANES
    wide = wide_of(tiles)
    last = tiles // wide - 1
    zero = jnp.zeros((rows, LANES), F32)
    for var in range(5):
        fy_ref[var, 0] = zero
        fy_ref[var, tiles + 1] = zero
    own = slice(SUB, SUB + rows)

    def store(t, grads):
        cut = pl.ds(pl.multiple_of(t * LANES, LANES), LANES)
        state = [state_ref[n, :, cut] for n in range(5)]
        u = [prim[a, t + 1, own, :] for a in range(3)]
        for var, f in enumerate(convective(state, u, press[t], 1)):
            scale = viscosity * (conduction if var == 4 else 1.0) / 60.0
            fy_ref[var, t + 1] = f - scale * grads(var - 1) if var else f

    def body(step, carry):
        t0 = step * wide
        inner, end = lane_differences(
            lhs, operator, lambda var, j: prim[var, t0 + j + 1, own, :], wide, 4, step, last)
        for j in range(wide):
            store(t0 + j, lambda var: inner(var, j))
        store(jnp.where(step == last, tiles - 1, t0), end)
        return carry

    lax.fori_loop(0, last + 1, body, 0)


def volume_kernel(state_ref, adjoint, fy, xd, operator, res_ref, sum_ref, lhs):
    refs = parts_of(state_ref)
    rows, cols = state_ref.shape[1:]
    row_tiles, tiles = rows // SUB, cols // LANES
    wide = wide_of(tiles)
    last = tiles // wide - 1

    def body(step, accs):
        t0 = step * wide
        accs = list(accs)
        inner, end = lane_differences(lhs, operator, lambda var, j: fy[var, t0 + j + 1], wide, 5, step, last)
        at_end = jnp.where(step == last, tiles - 1, t0)
        for var in range(5):
            for j in range(wide):
                t = t0 + j
                r = xd[var, t] + inner(var, j) * (1.0 / 60.0)
                res_ref[var, t] = r
                accs[j % 2] = accs[j % 2] + adjoint[var, :, pl.ds(pl.multiple_of(t * LANES, LANES), LANES)] * r
        for var in range(5):
            r = xd[var, at_end] + end(var) * (1.0 / 60.0)
            change = r - res_ref[var, at_end]
            res_ref[var, at_end] = r
            accs[var % 2] = accs[var % 2] + adjoint[var, :, pl.ds(pl.multiple_of(at_end * LANES, LANES), LANES)] * change
        return tuple(accs)

    zero = jnp.zeros((rows, LANES), F32)
    one, two = lax.fori_loop(0, last + 1, body, (zero, zero))
    both = one + two
    acc = both[0:SUB]
    for rt in range(1, row_tiles):
        acc = acc + both[rt * SUB:(rt + 1) * SUB]
    weight = jnp.where(tile_iota(1) == LANES - 1, penalty, 0.0)
    for rt in range(row_tiles):
        own = slice(rt * SUB, (rt + 1) * SUB)
        for var, x in enumerate(load_state(refs, rt, tiles - 1)):
            extra = weight * x
            res_ref[var, tiles - 1, own, :] = res_ref[var, tiles - 1, own, :] + extra
            acc = acc + adjoint[var, own, (tiles - 1) * LANES:] * extra
    sum_ref[...] = acc


def received(chip, across, t):
    odd = lax.rem(lax.axis_index("line"), 2) == 1
    at = pl.ds(pl.multiple_of(t * LANES, LANES), LANES)
    near = [chip[n, :, at] for n in range(4)]
    far = [across[n, :, at] for n in range(4)]
    below = unpack([jnp.where(odd, a, b) for a, b in zip(near, far)], True)
    above = unpack([jnp.where(odd, b, a) for a, b in zip(near, far)], False)
    return below, above


def border_sum_kernel(chip, across, slots, mix, adjoint, total, column_ref, sum_ref):
    rows, cols = adjoint.shape[1:]
    row_tiles, tiles = rows // SUB, cols // LANES

    def body(step, accs):
        accs = list(accs)
        for j in range(2):
            t = step * 2 + j
            at = pl.ds(pl.multiple_of(t * LANES, LANES), LANES)
            below, above = received(chip, across, t)
            for var in range(5):
                accs[j] = accs[j] + adjoint[var, 0:SUB, at] * below[var]
                accs[2 + j] = accs[2 + j] + adjoint[var, rows - SUB:rows, at] * above[var]
        return tuple(accs)

    zero = jnp.zeros((SUB, LANES), F32)
    accs = lax.fori_loop(0, tiles // 2, body, (zero,) * 4)
    acc = (total[...] + accs[0]) + (accs[1] + accs[2]) + accs[3]
    lane = tile_iota(1)
    target = slots[0] * mix[0]
    for m in range(1, slots.shape[0]):
        target = target + slots[m] * mix[m]
    step = slot_width(row_tiles)
    while step < LANES:
        target = target + pltpu.roll(target, step, 1)
        step *= 2
    for var in range(5):
        for rt in range(row_tiles):
            own = slice(rt * SUB, (rt + 1) * SUB)
            moved = pltpu.roll(target, LANES - 1 - (var * row_tiles + rt), 1)
            extra = jnp.where(lane == LANES - 1, -penalty * moved, 0.0)
            column_ref[var, own, :] = extra
            acc = acc + adjoint[var, own, (tiles - 1) * LANES:tiles * LANES] * extra
    points = rows * lax.axis_size("line") * cols
    sum_ref[...] = jnp.full((SUB, LANES), jnp.sum(acc) / points)


def border_kernel(chip, across, column, res, out_ref, stage, sems):
    rows, cols = stage.shape[1:]
    row_tiles, tiles = rows // SUB, cols // LANES

    def body(t, carry):
        at = pl.ds(pl.multiple_of(t * LANES, LANES), LANES)
        below, above = received(chip, across, t)
        for var in range(5):
            for rt in range(row_tiles):
                r = res[var, t, rt * SUB:(rt + 1) * SUB, :]
                for there, extra in ((0, below[var]), (row_tiles - 1, above[var])):
                    if rt == there:
                        r = r + extra
                stage[var, rt * SUB:(rt + 1) * SUB, at] = r
        return carry

    parts = 4
    size = tiles // parts
    copies = []
    for n in range(parts - 1, -1, -1):
        lax.fori_loop(n * size, (n + 1) * size, body, 0, unroll=2)
        if n == parts - 1:
            cut = slice((tiles - 1) * LANES, tiles * LANES)
            for var in range(5):
                stage[var, :, cut] = stage[var, :, cut] + column[var]
        cut = pl.ds(n * size * LANES, size * LANES)
        copies.append(pltpu.make_async_copy(stage.at[:, :, cut], out_ref.at[:, :, cut], sems.at[n]))
        copies[-1].start()
    for c in copies:
        c.wait()


def total_kernel(*refs):
    total = refs[0][...]
    for x in refs[1:-1]:
        total = total + x[...]
    refs[-1][0] = total[0, 0]


def per_device(density, momentum, energy, adjoint, partners, counts, orient):
    rows, cols = density.shape[1:]
    row_tiles, tiles = rows // SUB, cols // LANES
    lines, blocks = lax.axis_size("line"), lax.axis_size("blk")
    state = (density[0], momentum[0], energy[0])
    shape = jax.ShapeDtypeStruct
    pieces = -(-blocks * slot_width(row_tiles) // LANES)
    packed = shape((4, SUB, cols), F32)
    flat = shape((pieces, SUB, LANES), F32)
    anywhere = pl.BlockSpec(memory_space=pl.ANY)
    in_hbm = pl.BlockSpec(memory_space=pltpu.HBM)
    dma = pltpu.SemaphoreType.DMA

    def cost(micros):
        return pl.CostEstimate(flops=micros * 10**6, bytes_accessed=micros * 3 * 10**6, transcendentals=0)

    pad = pltpu.VMEM((4, 9, 3 * SUB, LANES), F32)
    send_far, slots, held = pl.pallas_call(
        pack_kernel, out_shape=[packed, flat, shape((5, rows, cols), F32)],
        in_specs=[in_hbm] * 3, out_specs=[whole()] * 3,
        scratch_shapes=[pad, dma((2 * row_tiles, 5))],
        compiler_params=params(), cost_estimate=cost(2),
    )(*[pltpu.with_memory_space_constraint(x, pltpu.HBM) for x in state])
    far = lax.ppermute(send_far, "line", [p for i in range(1, lines - 1, 2) for p in ((i, i + 1), (i + 1, i))])
    rounds = [slots]
    hop = 1
    while hop < blocks:
        got = lax.ppermute(rounds[-1], "blk", [(i, i ^ hop) for i in range(blocks)])
        rounds.append(rounds[-1] + got)
        hop *= 2
    slots = rounds[-1]

    operator = jnp.asarray(line_operator(cols))

    def lhs_of(count):
        return pltpu.VMEM((wide_of(tiles) * count * rows, 2 * PIECES * LANES), jnp.bfloat16)

    count_row = lax.pad(counts, jnp.int32(0), [(0, LANES - 1, 0)]).reshape(1, LANES)
    prim, press, xd, send_near, mix = pl.pallas_call(
        first_kernel,
        out_shape=[shape((4, tiles + 2, rows + 2 * SUB, LANES), F32), shape((tiles, rows, LANES), F32),
                   shape((5, tiles, rows, LANES), F32), packed, flat],
        in_specs=[whole()] * 4, out_specs=[whole()] * 5,
        scratch_shapes=[
            pltpu.VMEM((CHUNK, 5, rows + 3 * SUB, LANES), F32),
            pltpu.VMEM((2, row_tiles + 1, 4, SUB, LANES), F32),
        ],
        compiler_params=params(), cost_estimate=cost(3),
    )(held, count_row, partners, orient)
    near = lax.ppermute(send_near, "line", [(i, i ^ 1) for i in range(lines)])
    fy = pl.pallas_call(
        second_kernel, out_shape=shape((5, tiles + 2, rows, LANES), F32),
        in_specs=[whole()] * 4, out_specs=whole(), scratch_shapes=[lhs_of(4)],
        compiler_params=params(), cost_estimate=cost(2),
    )(held, prim, press, operator)
    res, total = pl.pallas_call(
        volume_kernel,
        out_shape=[shape((5, tiles, rows, LANES), F32), shape((SUB, LANES), F32)],
        in_specs=[whole()] * 5, out_specs=[whole()] * 2,
        scratch_shapes=[lhs_of(5)], compiler_params=params(), cost_estimate=cost(2),
    )(held, adjoint[0], fy, xd, operator)
    column, part = pl.pallas_call(
        border_sum_kernel,
        out_shape=[shape((5, rows, LANES), F32), shape((SUB, LANES), F32)],
        in_specs=[whole()] * 6, out_specs=[whole()] * 2, compiler_params=params(), cost_estimate=cost(1),
    )(near, far, slots, mix, adjoint[0], total)
    result = pl.pallas_call(
        border_kernel, out_shape=shape((5, rows, cols), F32),
        in_specs=[whole()] * 4, out_specs=anywhere,
        scratch_shapes=[pltpu.VMEM((5, rows, cols), F32), dma((4,))],
        compiler_params=params(), cost_estimate=cost(2),
    )(near, far, column, res)
    if lines <= 4:
        parts = [part]
        for n in range(1, lines):
            parts.append(lax.ppermute(part, "line", [(i, i ^ n) for i in range(lines)]))
        correction = pl.pallas_call(
            total_kernel, out_shape=shape((1,), F32), in_specs=[whole()] * lines,
            out_specs=pl.BlockSpec(memory_space=pltpu.SMEM), compiler_params=params(),
        )(*parts)
    else:
        correction = lax.psum(part, "line")[0, 0:1]
    return result[None], correction


def solution(mesh):
    return jax.shard_map(
        per_device,
        mesh=mesh,
        in_specs=(
            P("blk", "line", None),
            P("blk", None, "line", None),
            P("blk", "line", None),
            P("blk", None, "line", None),
            P("blk", None),
            P("blk"),
            P("blk", None),
        ),
        out_specs=(P("blk", None, "line", None), P("blk")),
        check_vma=False,
    )
```

```python
import jax
import jax.numpy as jnp
import numpy as np
from jax import lax
from jax.experimental import pallas as pl
from jax.experimental.pallas import tpu as pltpu
from jax.sharding import PartitionSpec as P


STENCIL = (0.75, -0.15, 1.0 / 60.0)
gamma_less = 0.4
viscosity = 0.5
conduction = 1.5
penalty = 4.0
LANES = 128
SUB = 8
CHUNK = 4
WIDE = 16
PIECES = 3
F32 = jnp.float32
VMEM_LIMIT = 20 * 1024 * 1024

_ONE = {k: STENCIL[k - 1] for k in (1, 2, 3)}
_ONE.update({-k: -STENCIL[k - 1] for k in (1, 2, 3)})
TWICE = [sum(_ONE[a] * _ONE[b] for a in _ONE for b in _ONE if a + b == m) for m in range(7)]


def tile_iota(axis):
    return lax.broadcasted_iota(jnp.int32, (SUB, LANES), axis)


def coefficients(index, extent):
    inside = (index >= 0) & (index < extent)
    end = (index == 0) | (index == extent - 1)
    second = (index == 1) | (index == extent - 2)
    fourth = (index == 2) | (index == extent - 3)
    one = jnp.where(fourth, 2.0 / 3.0, jnp.where(second, 0.5, jnp.where(end, 1.0, STENCIL[0])))
    two = jnp.where(fourth, -1.0 / 12.0, jnp.where(second | end, 0.0, STENCIL[1]))
    three = jnp.where(fourth | second | end, 0.0, STENCIL[2])
    point = jnp.where(index == 0, -1.0, jnp.where(index == extent - 1, 1.0, 0.0))
    return [jnp.where(inside, c, 0.0).astype(F32) for c in (one, two, three, point)]


def parts_of(state):
    return state.at[0], state.at[1:4], state.at[4]


def load_state(refs, rt, t):
    density, momentum, energy = refs
    rows = slice(rt * SUB, (rt + 1) * SUB)
    cols = pl.ds(t * LANES if isinstance(t, int) else pl.multiple_of(t * LANES, LANES), LANES)
    return [density[rows, cols]] + [momentum[a, rows, cols] for a in range(3)] + [energy[rows, cols]]


def primitive_of(state):
    rho, m0, m1, m2, e = state
    inv = 1.0 / rho
    u = [m0 * inv, m1 * inv, m2 * inv]
    p = gamma_less * (e - 0.5 * (m0 * u[0] + m1 * u[1] + m2 * u[2]))
    return u, p, p * inv


def convective(state, u, p, d):
    n = u[d]
    out = [state[1 + d]]
    for a in range(3):
        f = state[1 + a] * n
        out.append(f + p if a == d else f)
    out.append((state[4] + p) * n)
    return out


def contribution(state, up, pad):
    u, p, temp = primitive_of(state)
    conv = convective(state, u, p, 0)
    middle = slice(SUB, 2 * SUB)
    for n, x in enumerate(conv + u + [temp]):
        pad[n, middle, :] = x
    sign = -1.0 if up else 1.0

    def shifted(n, m):
        start = 2 * SUB - m if up else m
        return pad[n, start:start + SUB, :]

    out = []
    for var in range(5):
        acc = None
        for m in (1, 2, 3):
            term = shifted(var, m) * (sign * STENCIL[m - 1])
            acc = term if acc is None else acc + term
        if var:
            scale = -viscosity * (conduction if var == 4 else 1.0)
            for m in range(1, 7):
                acc = acc + shifted(4 + var, m) * (scale * TWICE[m])
        out.append(acc)
    return place_mass(out, up)


def place_mass(out, up):
    row = tile_iota(0)
    mass, first, second = out[0], out[1], out[2]
    if up:
        first = jnp.where(row >= 6, pltpu.roll(mass, 6, 0), first)
        second = jnp.where(row == 6, pltpu.roll(mass, 4, 0), second)
    else:
        first = jnp.where(row < 2, pltpu.roll(mass, 3, 0), first)
        second = jnp.where(row == 0, pltpu.roll(mass, 1, 0), second)
    return [first, second, out[3], out[4]]


def unpack(tiles, up):
    row = tile_iota(0)
    first, second, third, fourth = tiles
    if up:
        mass = jnp.where(row < 2, pltpu.roll(first, 2, 0), 0.0) + jnp.where(row == 2, pltpu.roll(second, 4, 0), 0.0)
        keep = row < 6
    else:
        mass = jnp.where((row == 5) | (row == 6), pltpu.roll(first, 5, 0), 0.0) + jnp.where(
            row == 7, pltpu.roll(second, 7, 0), 0.0)
        keep = row >= 2
    return [mass] + [jnp.where(keep, x, 0.0) for x in (first, second, third, fourth)]


def side_of(refs, up, out_ref, rt, first, last, pad):
    ways = pad.shape[0]

    def body(step, carry):
        for j in range(ways):
            t = step * ways + j
            cols = pl.ds(pl.multiple_of(t * LANES, LANES), LANES)
            for n, x in enumerate(contribution(load_state(refs, rt, t), up, pad.at[j])):
                out_ref[n, :, cols] = x
        return carry

    lax.fori_loop(first // ways, last // ways, body, 0)


def clear(pad):
    zero = jnp.zeros((SUB, LANES), F32)
    for j in range(pad.shape[0]):
        for n in range(pad.shape[1]):
            pad[j, n, 0:SUB, :] = zero
            pad[j, n, 2 * SUB:3 * SUB, :] = zero


def by_parity(up_when, run):
    odd = lax.rem(lax.axis_index("line"), 2)

    @pl.when(odd == up_when)
    def _():
        run(True)

    @pl.when(odd != up_when)
    def _():
        run(False)


def pack_kernel(density, momentum, energy, out_ref, slots, state_ref, pad, sems):
    rows, cols = density.shape
    row_tiles, tiles = rows // SUB, cols // LANES
    up = lax.rem(lax.axis_index("line"), 2) == 1
    mine = jnp.where(up, row_tiles - 1, 0)
    sources = [density] + [momentum.at[a] for a in range(3)] + [energy]
    halves = 2
    part = cols // halves

    def fetch(x, n, tile, h, sem):
        at = pl.ds(pl.multiple_of(tile * SUB, SUB), SUB)
        cut = pl.ds(h * part, part)
        return pltpu.make_async_copy(x.at[at, cut], state_ref.at[n, at, cut], sem)

    needed = [[fetch(x, n, mine, h, sems.at[h, n]) for n, x in enumerate(sources)] for h in range(halves)]
    rest = [fetch(x, n, jnp.where(mine == 0, k, k - 1), h, sems.at[halves * k + h, n])
            for k in range(1, row_tiles) for h in range(halves) for n, x in enumerate(sources)]
    for c in sum(needed, []) + rest:
        c.start()
    clear(pad)
    refs = parts_of(state_ref)
    for h in range(halves):
        for c in needed[h]:
            c.wait()
        by_parity(1, lambda up_side: side_of(
            refs, up_side, out_ref, row_tiles - 1 if up_side else 0, h * tiles // halves, (h + 1) * tiles // halves, pad))
    for c in rest:
        c.wait()
    width = slot_width(row_tiles)
    per = LANES // width
    block = lax.axis_index("blk")
    lane = tile_iota(1)
    base = lax.rem(block, per) * width
    value = jnp.zeros((SUB, LANES), F32)
    for rt in range(row_tiles):
        for var in range(5):
            x = state_ref[var, rt * SUB:(rt + 1) * SUB, 0:LANES][:, 0:1]
            value = jnp.where(lane == base + (var * row_tiles + rt), x, value)
    for n in range(slots.shape[0]):
        slots[n] = jnp.where(block // per == n, value, 0.0)


def slot_width(row_tiles):
    width = 1
    while width < 5 * row_tiles:
        width *= 2
    return width


def whole():
    return pl.BlockSpec(memory_space=pltpu.VMEM)


def params():
    return pltpu.CompilerParams(vmem_limit_bytes=VMEM_LIMIT)


def line_operator(cols):
    out = np.zeros((3, 2 * LANES, LANES), np.float32)
    for n, start in enumerate((0, LANES, cols - LANES)):
        for lane in range(LANES):
            at = start + lane
            edge = min(at, cols - 1 - at)
            if edge == 0:
                terms = {0: -60, 1: 60} if at == 0 else {0: 60, -1: -60}
            else:
                half = {1: (30,), 2: (40, -5)}.get(edge, (45, -9, 1))
                terms = {sign * (k + 1): sign * c for k, c in enumerate(half) for sign in (1, -1)}
            for offset, c in terms.items():
                out[n, (lane + offset) % (2 * LANES), lane] = c
    return np.tile(out, (1, PIECES, 1)).astype(jnp.bfloat16)


def split(x):
    pieces = []
    for _ in range(PIECES):
        piece = x.astype(jnp.bfloat16)
        pieces.append(piece)
        x = x - piece.astype(F32)
    return pieces


def wide_of(tiles):
    return max(w for w in range(1, WIDE + 1) if tiles % w == 0 and 2 * w <= tiles)


def lane_differences(lhs, operator, tile_of, wide, count, step, last):
    rows = lhs.shape[0] // (wide * count)
    lane = lax.broadcasted_iota(jnp.int32, (rows, LANES), 1)
    for var in range(count):
        for j in range(wide):
            at = slice((j * count + var) * rows, (j * count + var + 1) * rows)
            cur = split(tile_of(var, j))
            mix = split(jnp.where(lane < LANES // 2, tile_of(var, j + 1), tile_of(var, j - 1)))
            for n in range(PIECES):
                lhs[at, 2 * n * LANES:(2 * n + 1) * LANES] = cur[n]
                lhs[at, (2 * n + 1) * LANES:(2 * n + 2) * LANES] = mix[n]
    out = jnp.dot(lhs[...], operator[1], preferred_element_type=F32)
    which = jnp.where(step == 0, 0, jnp.where(step == last, 2, 1))
    size = count * rows
    start = pl.multiple_of(jnp.where(step == last, (wide - 1) * size, 0), size)
    end = jnp.dot(lhs[pl.ds(start, size), :], operator[which], preferred_element_type=F32)
    return (lambda var, j: out[(j * count + var) * rows:(j * count + var + 1) * rows],
            lambda var: end[var * rows:(var + 1) * rows])


def apply(weights, at):
    one, two, three, point = weights
    return one * (at(1) - at(-1)) + two * (at(2) - at(-2)) + three * (at(3) - at(-3)) + point * at(0)


def interior(at):
    one, two, three = STENCIL
    return one * (at(1) - at(-1)) + two * (at(2) - at(-2)) + three * (at(3) - at(-3))


def first_kernel(state_ref, counts, partners, orient,
                 prim, press, xd_ref, near_ref, mix_ref, fx, xcoef):
    refs = parts_of(state_ref)
    rows, cols = state_ref.shape[1:]
    row_tiles, tiles = rows // SUB, cols // LANES
    line = lax.axis_index("line")
    extent = rows * lax.axis_size("line")
    zero = jnp.zeros((SUB, LANES), F32)
    for g in range(row_tiles + 1):
        for c, w in enumerate(coefficients(line * rows - 3 + g * SUB + tile_iota(0), extent)):
            xcoef[0, g, c] = w
    for r in range(row_tiles):
        for c, w in enumerate(coefficients(line * rows + r * SUB + tile_iota(0), extent)):
            xcoef[1, r, c] = w
    for var in range(4):
        for r in range(row_tiles + 2):
            prim[var, 0, r * SUB:(r + 1) * SUB, :] = zero
            prim[var, tiles + 1, r * SUB:(r + 1) * SUB, :] = zero
    for j in range(CHUNK):
        for var in range(5):
            for r in range(row_tiles + 3):
                fx[j, var, r * SUB:(r + 1) * SUB, :] = zero
    odd = lax.rem(line, 2)
    beyond = pl.multiple_of((rows + SUB) * (1 - odd), SUB)

    def body(step, carry):
        for j in range(CHUNK):
            t = step * CHUNK + j
            flux = []
            for rt in range(row_tiles):
                state = load_state(refs, rt, t)
                u, p, temp = primitive_of(state)
                at = slice((rt + 1) * SUB, (rt + 2) * SUB)
                for var, x in enumerate(u + [temp]):
                    prim[var, t + 1, at, :] = x
                press[t, rt * SUB:(rt + 1) * SUB, :] = p
                flux.append(convective(state, u, p, 0))
            for var in range(4):
                prim[var, t + 1, 0:SUB, :] = zero
                prim[var, t + 1, (row_tiles + 1) * SUB:(row_tiles + 2) * SUB, :] = zero
            for var in range(4):
                scale = -viscosity * (conduction if var == 3 else 1.0)
                for g in range(row_tiles + 1):
                    base = SUB - 3 + g * SUB
                    at = lambda k: prim[var, t + 1, base + k:base + k + SUB, :]
                    if 0 < g < row_tiles:
                        d = interior(at)
                    else:
                        d = apply([xcoef[0, g, c] for c in range(4)], at)
                    fx[j, var + 1, (g + 1) * SUB:(g + 2) * SUB, :] = scale * d
            for rt in range(row_tiles):
                place = slice(11 + rt * SUB, 11 + (rt + 1) * SUB)
                for var, f in enumerate(flux[rt]):
                    fx[j, var, place, :] = fx[j, var, place, :] + f if var else f
            for var in range(5):
                for rt in range(row_tiles):
                    w = [xcoef[1, rt, c] for c in range(4)]
                    base = 11 + rt * SUB
                    xd_ref[var, t, rt * SUB:(rt + 1) * SUB, :] = apply(
                        w, lambda k: fx[j, var, base + k:base + k + SUB, :])
            out = [interior(lambda k: fx[j, var, pl.ds(beyond + (3 + k), SUB), :]) for var in range(5)]
            cut = pl.ds(pl.multiple_of(t * LANES, LANES), LANES)
            for n, (a, b) in enumerate(zip(place_mass(out, True), place_mass(out, False))):
                near_ref[n, :, cut] = jnp.where(odd == 1, b, a) if n < 2 else a
        return carry

    lax.fori_loop(0, tiles // CHUNK, body, 0)

    width = slot_width(row_tiles)
    per = LANES // width
    lane = tile_iota(1)

    def spread(ref, k):
        return jnp.broadcast_to(ref[0:1, k:k + 1], (SUB, LANES))

    count = spread(counts, 0)
    share = 1.0 / count.astype(F32)
    flipped = (lane % width) // row_tiles == 2
    for n in range(mix_ref.shape[0]):
        weight = zero
        for k in range(partners.shape[1]):
            turn = 1.0 - 2.0 * spread(orient, k).astype(F32)
            hit = (lane // width + n * per == spread(partners, k)) & (k < count)
            weight = weight + jnp.where(hit, share * jnp.where(flipped, turn, 1.0), 0.0)
        mix_ref[n] = weight


def second_kernel(state_ref, prim, press, operator, fy_ref, lhs):
    rows, cols = state_ref.shape[1:]
    tiles = cols // LANES
    wide = wide_of(tiles)
    last = tiles // wide - 1
    zero = jnp.zeros((rows, LANES), F32)
    for var in range(5):
        fy_ref[var, 0] = zero
        fy_ref[var, tiles + 1] = zero
    own = slice(SUB, SUB + rows)

    def store(t, grads):
        cut = pl.ds(pl.multiple_of(t * LANES, LANES), LANES)
        state = [state_ref[n, :, cut] for n in range(5)]
        u = [prim[a, t + 1, own, :] for a in range(3)]
        for var, f in enumerate(convective(state, u, press[t], 1)):
            scale = viscosity * (conduction if var == 4 else 1.0) / 60.0
            fy_ref[var, t + 1] = f - scale * grads(var - 1) if var else f

    def body(step, carry):
        t0 = step * wide
        inner, end = lane_differences(
            lhs, operator, lambda var, j: prim[var, t0 + j + 1, own, :], wide, 4, step, last)
        for j in range(wide):
            store(t0 + j, lambda var: inner(var, j))
        store(jnp.where(step == last, tiles - 1, t0), end)
        return carry

    lax.fori_loop(0, last + 1, body, 0)


def volume_kernel(state_ref, adjoint, fy, xd, operator, res_ref, sum_ref, lhs):
    refs = parts_of(state_ref)
    rows, cols = state_ref.shape[1:]
    row_tiles, tiles = rows // SUB, cols // LANES
    wide = wide_of(tiles)
    last = tiles // wide - 1

    def body(step, accs):
        t0 = step * wide
        accs = list(accs)
        inner, end = lane_differences(lhs, operator, lambda var, j: fy[var, t0 + j + 1], wide, 5, step, last)
        at_end = jnp.where(step == last, tiles - 1, t0)
        for var in range(5):
            for j in range(wide):
                t = t0 + j
                r = xd[var, t] + inner(var, j) * (1.0 / 60.0)
                res_ref[var, t] = r
                accs[j % 2] = accs[j % 2] + adjoint[var, :, pl.ds(pl.multiple_of(t * LANES, LANES), LANES)] * r
        for var in range(5):
            r = xd[var, at_end] + end(var) * (1.0 / 60.0)
            change = r - res_ref[var, at_end]
            res_ref[var, at_end] = r
            accs[var % 2] = accs[var % 2] + adjoint[var, :, pl.ds(pl.multiple_of(at_end * LANES, LANES), LANES)] * change
        return tuple(accs)

    zero = jnp.zeros((rows, LANES), F32)
    one, two = lax.fori_loop(0, last + 1, body, (zero, zero))
    both = one + two
    acc = both[0:SUB]
    for rt in range(1, row_tiles):
        acc = acc + both[rt * SUB:(rt + 1) * SUB]
    weight = jnp.where(tile_iota(1) == LANES - 1, penalty, 0.0)
    for rt in range(row_tiles):
        own = slice(rt * SUB, (rt + 1) * SUB)
        for var, x in enumerate(load_state(refs, rt, tiles - 1)):
            extra = weight * x
            res_ref[var, tiles - 1, own, :] = res_ref[var, tiles - 1, own, :] + extra
            acc = acc + adjoint[var, own, (tiles - 1) * LANES:] * extra
    sum_ref[...] = acc


def received(chip, across, t):
    odd = lax.rem(lax.axis_index("line"), 2) == 1
    at = pl.ds(pl.multiple_of(t * LANES, LANES), LANES)
    near = [chip[n, :, at] for n in range(4)]
    far = [across[n, :, at] for n in range(4)]
    below = unpack([jnp.where(odd, a, b) for a, b in zip(near, far)], True)
    above = unpack([jnp.where(odd, b, a) for a, b in zip(near, far)], False)
    return below, above


def border_sum_kernel(chip, across, slots, mix, adjoint, total, column_ref, sum_ref):
    rows, cols = adjoint.shape[1:]
    row_tiles, tiles = rows // SUB, cols // LANES

    def body(step, accs):
        accs = list(accs)
        for j in range(4):
            t = step * 4 + j
            at = pl.ds(pl.multiple_of(t * LANES, LANES), LANES)
            below, above = received(chip, across, t)
            for var in range(5):
                accs[j] = accs[j] + (adjoint[var, 0:SUB, at] * below[var] + adjoint[var, rows - SUB:rows, at] * above[var])
        return tuple(accs)

    zero = jnp.zeros((SUB, LANES), F32)
    accs = lax.fori_loop(0, tiles // 4, body, (zero,) * 4)
    acc = total[...] + ((accs[0] + accs[1]) + (accs[2] + accs[3]))
    lane = tile_iota(1)
    width = slot_width(row_tiles)
    target = slots[0] * mix[0]
    for m in range(1, slots.shape[0]):
        target = target + slots[m] * mix[m]
    for var in range(5):
        for rt in range(row_tiles):
            own = slice(rt * SUB, (rt + 1) * SUB)
            mine = lane % width == var * row_tiles + rt
            value = jnp.sum(jnp.where(mine, target, 0.0), axis=1, keepdims=True)
            extra = jnp.where(lane == LANES - 1, -penalty * value, 0.0)
            column_ref[var, own, :] = extra
            acc = acc + adjoint[var, own, (tiles - 1) * LANES:tiles * LANES] * extra
    points = rows * lax.axis_size("line") * cols
    sum_ref[...] = jnp.full((SUB, LANES), jnp.sum(acc) / points)


def border_kernel(chip, across, column, res, out_ref, stage, sems):
    rows, cols = stage.shape[1:]
    row_tiles, tiles = rows // SUB, cols // LANES

    def body(t, carry):
        at = pl.ds(pl.multiple_of(t * LANES, LANES), LANES)
        below, above = received(chip, across, t)
        for var in range(5):
            for rt in range(row_tiles):
                r = res[var, t, rt * SUB:(rt + 1) * SUB, :]
                for there, extra in ((0, below[var]), (row_tiles - 1, above[var])):
                    if rt == there:
                        r = r + extra
                stage[var, rt * SUB:(rt + 1) * SUB, at] = r
        return carry

    parts = 4
    size = tiles // parts
    copies = []
    for n in range(parts - 1, -1, -1):
        lax.fori_loop(n * size, (n + 1) * size, body, 0, unroll=2)
        if n == parts - 1:
            cut = slice((tiles - 1) * LANES, tiles * LANES)
            for var in range(5):
                stage[var, :, cut] = stage[var, :, cut] + column[var]
        cut = pl.ds(n * size * LANES, size * LANES)
        copies.append(pltpu.make_async_copy(stage.at[:, :, cut], out_ref.at[:, :, cut], sems.at[n]))
        copies[-1].start()
    for c in copies:
        c.wait()


def total_kernel(*refs):
    total = refs[0][...]
    for x in refs[1:-1]:
        total = total + x[...]
    refs[-1][0] = total[0, 0]


def per_device(density, momentum, energy, adjoint, partners, counts, orient):
    rows, cols = density.shape[1:]
    row_tiles, tiles = rows // SUB, cols // LANES
    lines, blocks = lax.axis_size("line"), lax.axis_size("blk")
    state = (density[0], momentum[0], energy[0])
    shape = jax.ShapeDtypeStruct
    pieces = -(-blocks * slot_width(row_tiles) // LANES)
    packed = shape((4, SUB, cols), F32)
    flat = shape((pieces, SUB, LANES), F32)
    anywhere = pl.BlockSpec(memory_space=pl.ANY)
    in_hbm = pl.BlockSpec(memory_space=pltpu.HBM)
    dma = pltpu.SemaphoreType.DMA

    def cost(micros):
        return pl.CostEstimate(flops=micros * 10**6, bytes_accessed=micros * 3 * 10**6, transcendentals=0)

    pad = pltpu.VMEM((4, 9, 3 * SUB, LANES), F32)
    send_far, slots, held = pl.pallas_call(
        pack_kernel, out_shape=[packed, flat, shape((5, rows, cols), F32)],
        in_specs=[in_hbm] * 3, out_specs=[whole()] * 3,
        scratch_shapes=[pad, dma((2 * row_tiles, 5))],
        compiler_params=params(), cost_estimate=cost(2),
    )(*[pltpu.with_memory_space_constraint(x, pltpu.HBM) for x in state])
    far = lax.ppermute(send_far, "line", [p for i in range(1, lines - 1, 2) for p in ((i, i + 1), (i + 1, i))])
    rounds = [slots]
    hop = 1
    while hop < blocks:
        got = lax.ppermute(rounds[-1], "blk", [(i, i ^ hop) for i in range(blocks)])
        rounds.append(rounds[-1] + got)
        hop *= 2
    slots = rounds[-1]

    operator = jnp.asarray(line_operator(cols))

    def lhs_of(count):
        return pltpu.VMEM((wide_of(tiles) * count * rows, 2 * PIECES * LANES), jnp.bfloat16)

    count_row = lax.pad(counts, jnp.int32(0), [(0, LANES - 1, 0)]).reshape(1, LANES)
    prim, press, xd, send_near, mix = pl.pallas_call(
        first_kernel,
        out_shape=[shape((4, tiles + 2, rows + 2 * SUB, LANES), F32), shape((tiles, rows, LANES), F32),
                   shape((5, tiles, rows, LANES), F32), packed, flat],
        in_specs=[whole()] * 4, out_specs=[whole()] * 5,
        scratch_shapes=[
            pltpu.VMEM((CHUNK, 5, rows + 3 * SUB, LANES), F32),
            pltpu.VMEM((2, row_tiles + 1, 4, SUB, LANES), F32),
        ],
        compiler_params=params(), cost_estimate=cost(3),
    )(held, count_row, partners, orient)
    near = lax.ppermute(send_near, "line", [(i, i ^ 1) for i in range(lines)])
    fy = pl.pallas_call(
        second_kernel, out_shape=shape((5, tiles + 2, rows, LANES), F32),
        in_specs=[whole()] * 4, out_specs=whole(), scratch_shapes=[lhs_of(4)],
        compiler_params=params(), cost_estimate=cost(2),
    )(held, prim, press, operator)
    res, total = pl.pallas_call(
        volume_kernel,
        out_shape=[shape((5, tiles, rows, LANES), F32), shape((SUB, LANES), F32)],
        in_specs=[whole()] * 5, out_specs=[whole()] * 2,
        scratch_shapes=[lhs_of(5)], compiler_params=params(), cost_estimate=cost(2),
    )(held, adjoint[0], fy, xd, operator)
    column, part = pl.pallas_call(
        border_sum_kernel,
        out_shape=[shape((5, rows, LANES), F32), shape((SUB, LANES), F32)],
        in_specs=[whole()] * 6, out_specs=[whole()] * 2, compiler_params=params(), cost_estimate=cost(1),
    )(near, far, slots, mix, adjoint[0], total)
    result = pl.pallas_call(
        border_kernel, out_shape=shape((5, rows, cols), F32),
        in_specs=[whole()] * 4, out_specs=anywhere,
        scratch_shapes=[pltpu.VMEM((5, rows, cols), F32), dma((4,))],
        compiler_params=params(), cost_estimate=cost(2),
    )(near, far, column, res)
    if lines <= 4:
        parts = [part]
        for n in range(1, lines):
            parts.append(lax.ppermute(part, "line", [(i, i ^ n) for i in range(lines)]))
        correction = pl.pallas_call(
            total_kernel, out_shape=shape((1,), F32), in_specs=[whole()] * lines,
            out_specs=pl.BlockSpec(memory_space=pltpu.SMEM), compiler_params=params(),
        )(*parts)
    else:
        correction = lax.psum(part, "line")[0, 0:1]
    return result[None], correction


def solution(mesh):
    return jax.shard_map(
        per_device,
        mesh=mesh,
        in_specs=(
            P("blk", "line", None),
            P("blk", None, "line", None),
            P("blk", "line", None),
            P("blk", None, "line", None),
            P("blk", None),
            P("blk"),
            P("blk", None),
        ),
        out_specs=(P("blk", None, "line", None), P("blk")),
        check_vma=False,
    )
```
